512 devices in a mesh: ep: 16 (over y, core), tp: 32 (over z, x).
Axes of the slice: x: 4, y: 8, z: 8, core: 2. Of those that a mesh axis runs over, the one named last changes fastest.
Arguments:
- attn_out: bfloat16 [2048, 2048], P('ep'), may hold values from -6 to 6
- residual_in: bfloat16 [2048, 2048], P('ep'), may hold values from -6 to 6
- w_out: bfloat16 [2048, 2048], P(None, 'tp'), may hold values from -0.125 to 0.125
- gain_in: float32 [2048], replicated, may hold values from 0.1 to 1.9
- router_logits: float32 [2048, 8], P('ep'), may hold values from -8 to 8
- expert_ids: int32 [2048, 2], P('ep'), may hold values from 0 to 7, all different within a row; in each aligned block of 128 rows (0 to 127, 128 to 255, ...) at most 64 rows name the same one
- copy_of: int32 [16, 8], replicated, may hold values from 0 to 15, as said below
- w_gate: bfloat16 [16, 2048, 5632], P('ep', None, 'tp')
- w_up: bfloat16 [16, 2048, 5632], P('ep', None, 'tp')
- w_down: bfloat16 [16, 5632, 2048], P('ep', 'tp')
- gain_out: float32 [2048], replicated, may hold values from 0.1 to 1.9
Outputs:
- layer_out: bfloat16 [2048, 2048], P(('ep', 'tp'))
- next_input: bfloat16 [2048, 2048], P(('ep', 'tp'))
The draws below stay inside these ranges and needn't reach their ends.
Inputs may be any that keep to these rules, and one draw needn't show every extreme that they name: `expert_ids`: each row names 2 different experts. Within the rows of one ep group (aligned blocks of 128 rows) no expert is named by more than 64 rows, and in every draw some group has an expert named by exactly 64 rows. copy_of[s, e] is a copy of expert e, so different experts of one group go to different copies; copies of one expert carry equal weights.
All inputs are finite; a program needn't handle non-finite values.
Results may differ from the reference program's by a relative error of at most 0.019.
Values may be sent and summed in bfloat16 or wider, within the bound.
A program may use at most 64 MiB of HBM per device.

```python
import math
import jax
import jax.numpy as jnp
import numpy as np
from jax import lax

D = 2048
FF = 5632
E = 8
TOPK = 2
COPIES = 16
ROWS_DEV = 4
CAPG = 64
ROWS = 2048
N_EP = 16
N_TP = 32


def placement(key):
    place_key = jax.random.fold_in(key, 5)
    spare_key, shuffle_key = jax.random.split(place_key)
    spare_copies = jax.random.randint(spare_key, (COPIES - E,), 0, E).astype(jnp.int32)
    base_list = jnp.concatenate([jnp.arange(E, dtype=jnp.int32), spare_copies])
    return jax.random.permutation(shuffle_key, base_list)


def draw_copy_of(key, part):
    holders = placement(key)
    score_key = jax.random.fold_in(key, 9)
    scores = jax.random.randint(score_key, (N_EP, E, COPIES), 0, 4096).astype(jnp.int32)
    matches = holders[None, None, :] == jnp.arange(E, dtype=jnp.int32)[None, :, None]
    ranked = jnp.where(matches, scores * COPIES + jnp.arange(COPIES, dtype=jnp.int32)[None, None, :], -1)
    return lax.top_k(ranked, 1)[1][..., 0].astype(jnp.int32)


def copy_weights(key, salt, rows_count, cols_count, scale):
    holders = placement(key)
    experts = jax.random.normal(jax.random.fold_in(key, salt), (E, rows_count, cols_count), jnp.float32) * scale
    return experts[holders].astype(jnp.bfloat16)


def draw_w_gate(key, part):
    return copy_weights(key, 11, D, FF, D ** (-0.5))


def draw_w_up(key, part):
    return copy_weights(key, 13, D, FF, D ** (-0.5))


def draw_w_down(key, part):
    return copy_weights(key, 17, FF, D, 2.0 * FF ** (-0.5))


def steps_of(own_key, shape, cuts, smallest, largest):
    level = 1.0
    for dim, parts in cuts:
        draws = jax.random.uniform(jax.random.fold_in(jax.random.fold_in(own_key, 6), dim), (parts,), jnp.float32, smallest / len(cuts), largest / len(cuts))
        level = level * jnp.repeat(jnp.exp(draws), shape[dim] // parts).reshape((-1,) + (1,) * (len(shape) - 1 - dim))
    return level


def assign_block(key, own, number, rows, count, top, reach, slope):
    sequence = jax.random.permutation(key, count)
    crowded, common = portions_of(count, rows * top, reach, slope, True), portions_of(count, rows * top, reach, slope, False)
    places = jnp.arange(count)

    def named(lengths, offset_by):
        used = int((lengths > 0).sum())
        fixed = max(1, used // 4)
        passed = fixed + (places - fixed + offset_by * (used - fixed)) % max(1, count - fixed)
        return jnp.zeros((count,), jnp.int32).at[sequence[jnp.where(places < fixed, places, passed)]].set(jnp.asarray(lengths, jnp.int32))

    lengths = jnp.where(number % 4 == 0, named(crowded, number // 4), named(common, number - number // 4 - 1))
    mixed = jax.random.permutation(jax.random.fold_in(own, 3), count)
    source_of, sink = mixed[0:count // 2 * 2:2], mixed[1:count // 2 * 2:2]
    room = jnp.minimum(lengths[source_of] - 1, reach - lengths[sink]) // 2
    room = jnp.where((source_of == sequence[0]) | (sink == sequence[0]) | (lengths[sink] == 0), 0, jnp.maximum(room, 0))
    passed = jax.random.randint(jax.random.fold_in(own, 4), (count // 2,), 0, 1 << 20) % (room + 1)
    lengths = lengths.at[source_of].add(-passed).at[sink].add(passed)
    labels = jnp.searchsorted(jnp.cumsum(lengths), jnp.arange(rows * top), side="right").astype(jnp.int32)
    table = labels.reshape(top, rows).T
    table = table[jax.random.permutation(jax.random.fold_in(own, 1), rows)]
    offset_by = jax.random.randint(jax.random.fold_in(own, 2), (rows, 1), 0, top)
    return jnp.take_along_axis(table, (jnp.arange(top)[None, :] + offset_by) % top, axis=1)


def portions_of(amount, total, limit, lean, full):
    loads = [(1 << 20) // math.isqrt(grade ** lean) + 1 for grade in range(1, amount + 1)]
    largest = limit if full else min(limit, max(-(-total // amount), total * loads[0] // sum(loads)))
    least = 1 if total - largest >= amount - 1 else 0
    holding, spare = [largest] + [least] * (amount - 1), total - largest - least * (amount - 1)
    while spare > 0:
        movable = [i for i in range(1, amount) if holding[i] < largest] or [i for i in range(1, amount) if holding[i] < limit]
        mass, remaining = sum([loads[i] for i in movable]), spare
        for i in movable:
            more = min(limit - holding[i], max(1, remaining * loads[i] // mass), spare)
            holding[i] = holding[i] + more
            spare = spare - more
    return np.array(holding)


def scatter_about(key, extent, deviation, reach, cuts=(), held_as=jnp.bfloat16):
    entries = jax.random.normal(key, extent, jnp.float32) * deviation
    if len(cuts) > 0:
        entries = steps_of(key, extent, cuts, -0.22, 0.18) * entries
    return jnp.clip(entries, min=-reach, max=reach).astype(held_as)


def setup_inputs(seed: int = 0) -> dict:
    streams_of = jax.random.split(jax.random.key(seed), 12)
    attn_out = scatter_about(streams_of[0], (ROWS, D), 1.0, 6.0, ((0, 16),))
    residual_in = scatter_about(streams_of[1], (ROWS, D), 1.0, 6.0, ((0, 16),))
    w_out = scatter_about(streams_of[2], (D, D), D ** -0.5, 0.125, ((1, 32),))
    gain_in = jnp.clip(1.0 + 0.18 * jax.random.normal(streams_of[3], (D,), jnp.float32), 0.1, 1.9)
    router_logits = scatter_about(streams_of[4], (ROWS, E), 2.0, 8.0, ((0, 16),), jnp.float32)
    expert_ids_keys = jax.random.split(jax.random.fold_in(streams_of[5], 1), ROWS // (ROWS_DEV * N_TP))
    expert_ids_turns = jax.random.permutation(jax.random.fold_in(streams_of[5], 3), ROWS // (ROWS_DEV * N_TP))
    expert_ids = jax.vmap(lambda own, number: assign_block(jax.random.fold_in(streams_of[5], 2), own, number, ROWS_DEV * N_TP, E, TOPK, CAPG, 2))(expert_ids_keys, expert_ids_turns).reshape((ROWS, TOPK))
    copy_of = draw_copy_of(jax.random.fold_in(streams_of[11], 71), 0)
    w_gate = draw_w_gate(jax.random.fold_in(streams_of[11], 71), 0)
    w_up = draw_w_up(jax.random.fold_in(streams_of[11], 71), 0)
    w_down = draw_w_down(jax.random.fold_in(streams_of[11], 71), 0)
    gain_out = jnp.clip(1.0 + 0.18 * jax.random.normal(streams_of[10], (D,), jnp.float32), 0.1, 1.9)
    return {"attn_out": attn_out, "residual_in": residual_in, "w_out": w_out, "gain_in": gain_in, "router_logits": router_logits, "expert_ids": expert_ids, "copy_of": copy_of, "w_gate": w_gate, "w_up": w_up, "w_down": w_down, "gain_out": gain_out}


def rms_scale(values, gain):
    mean_square = lax.optimization_barrier(jnp.mean(values * values, axis=-1, keepdims=True))
    return values * lax.rsqrt(mean_square + 1e-06) * gain

def reference(attn_out, residual_in, w_out, gain_in, router_logits, expert_ids, copy_of, w_gate, w_up, w_down, gain_out):
    projected = jnp.dot(attn_out, w_out, preferred_element_type=jnp.float32).astype(jnp.bfloat16)
    carried = (residual_in.astype(jnp.float32) + projected.astype(jnp.float32)).astype(jnp.bfloat16)
    normed = rms_scale(carried.astype(jnp.float32), gain_in).astype(jnp.bfloat16)
    chosen = jnp.take_along_axis(router_logits, expert_ids, axis=1)
    gate_share = jax.nn.sigmoid(chosen - chosen[:, ::-1])
    group_rows = ROWS_DEV * N_TP
    capacity = group_rows // 2
    row_group = jnp.arange(ROWS, dtype=jnp.int32) // group_rows
    target = copy_of[row_group[:, None], expert_ids]
    copy_hits = (target[:, :, None] == jnp.arange(COPIES, dtype=jnp.int32)[None, None, :]).astype(jnp.int32)
    per_row = lax.optimization_barrier(jnp.sum(copy_hits, axis=1)).reshape(N_EP, group_rows, COPIES)
    before = (jnp.cumsum(per_row, axis=1) - per_row).reshape(ROWS, COPIES)
    position = lax.optimization_barrier(jnp.sum(copy_hits * before[:, None, :], axis=2))
    slot_flat = ((target * N_EP + row_group[:, None]) * capacity + position).astype(jnp.int32)
    row_numbers = jnp.broadcast_to(jnp.arange(ROWS, dtype=jnp.int32)[:, None], (ROWS, TOPK))
    total_slots = COPIES * N_EP * capacity
    slot_rows = jnp.zeros((total_slots,), jnp.int32).at[slot_flat.reshape(-1)].set(row_numbers.reshape(-1))
    slot_rows = slot_rows.reshape(COPIES, N_EP * capacity)

    def one_copy(inputs):
        rows_here, gate_weight, up_weight, down_weight = inputs
        inputs_here = normed[rows_here]
        gate_value = jnp.dot(inputs_here, gate_weight, preferred_element_type=jnp.float32)
        up_value = jnp.dot(inputs_here, up_weight, preferred_element_type=jnp.float32)
        hidden = (jax.nn.silu(gate_value) * up_value).astype(jnp.bfloat16)
        hidden_blocks = hidden.reshape(-1, N_TP, FF // N_TP).astype(jnp.float32)
        down_blocks = down_weight.reshape(N_TP, FF // N_TP, D).astype(jnp.float32)
        block_terms = jnp.einsum('snf,nfd->snd', hidden_blocks, down_blocks)
        rounded_terms = lax.optimization_barrier(block_terms.astype(jnp.bfloat16))
        return lax.optimization_barrier(jnp.sum(rounded_terms.astype(jnp.float32), axis=1)).astype(jnp.bfloat16)
    copy_outputs = lax.map(one_copy, (slot_rows, w_gate, w_up, w_down))
    flat_outputs = copy_outputs.reshape(total_slots, D)
    copy_out = flat_outputs[slot_flat]
    mixture = lax.optimization_barrier(jnp.sum(gate_share[:, :, None] * copy_out.astype(jnp.float32), axis=1))
    layer_out = (carried.astype(jnp.float32) + mixture).astype(jnp.bfloat16)
    next_input = rms_scale(layer_out.astype(jnp.float32), gain_out).astype(jnp.bfloat16)
    return (layer_out, next_input)
```

```python
import functools
import heapq

import jax
import jax.numpy as jnp
from jax import lax
from jax.experimental import pallas as pl
from jax.experimental.pallas import tpu as pltpu
from jax.sharding import PartitionSpec as P

MESH = pl.DeviceIdType.MESH
F32 = jnp.float32
BF16 = jnp.bfloat16
NX = 4
COLS = 64
GROUP = 128
CAP = 64
SIGNS = (1, -1)


def row_range(parts, part, sign, dist, count):
    start, size = parts[part]
    if 2 * dist == count:
        half = size // 2
        return (start, half) if sign > 0 else (start + half, half)
    return (start, size)


def ordered(sends, ready):
    rate, latency = 46500.0, 1.7
    heap, serial = [], 0
    for when, event in ready:
        heapq.heappush(heap, (when, serial, event))
        serial += 1
    done, free, waiting, ops = set(), {}, dict(sends), []

    def release(now):
        nonlocal serial
        for key in [k for k, v in waiting.items() if v[2] <= done]:
            link, size, _ = waiting.pop(key)
            begin = max(now, free.get(link, 0.0))
            free[link] = begin + size / rate
            ops.append(("start", key))
            heapq.heappush(heap, (free[link] + latency, serial, ("wait", key)))
            serial += 1

    release(0.0)
    while heap:
        now, _, event = heapq.heappop(heap)
        ops.append(event)
        done.add(event)
        release(now)
    assert not waiting
    return ops


def gather_plan(nz, nx, parts):
    count = {"z": nz, "x": nx}
    sends = {}
    for part, (first, second) in (("a", ("x", "z")), ("b", ("z", "x"))):
        for axis in (first, second):
            n = count[axis]
            for other in range(1 if axis == first else count[first]):
                for dist in range(1, n // 2 + 1):
                    for sign in SIGNS:
                        need = set()
                        if dist > 1:
                            need.add(("wait", (part, axis, sign, dist - 1, other)))
                        elif axis == second and other:
                            m = count[first]
                            if 2 * other <= m:
                                need.add(("wait", (part, first, 1, other, 0)))
                            if 2 * other >= m:
                                need.add(("wait", (part, first, -1, m - other, 0)))
                        size = row_range(parts, part, sign, dist, n)[1] * 256
                        sends[(part, axis, sign, dist, other)] = ((axis, sign), size, need)
    return list(sends), ordered(sends, [])


def reduce_plan(nz, nx, parts, step):
    count = {"z": nz, "x": nx}
    far = sorted(range(nz), key=lambda d: (-min(d, nz - d), d))
    chunk_at = [((i + 1) * step, ("chunk", dz)) for i, dz in enumerate(far)]
    sends = {}
    for part, (first, second) in (("a", ("z", "x")), ("b", ("x", "z"))):
        for axis in (first, second):
            n = count[axis]
            for other in range(count[second] if axis == first else 1):
                for dist in range(n // 2, 0, -1):
                    for sign in SIGNS:
                        offset = (sign * dist) % n
                        dz = offset if axis == "z" else other
                        need = {("chunk", dz)}
                        if 2 * dist < n:
                            need.add(("wait", (part, axis, sign, dist + 1, other)))
                        if axis == second:
                            for s in SIGNS:
                                need.add(("wait", (part, first, s, 1, offset)))
                        size = row_range(parts, part, sign, dist, n)[1] * 256
                        sends[(part, axis, sign, dist, other)] = ((axis, sign), size, need)
    return list(sends), ordered(sends, chunk_at), far


def iota(shape, dim):
    return lax.broadcasted_iota(jnp.int32, shape, dim)


def left_half(shape):
    return iota(shape, len(shape) - 1) < COLS


def swap(value):
    return pltpu.roll(value, COLS, value.ndim - 1)


def rank_before(hits):
    tri = (iota((GROUP, GROUP), 0) < iota((GROUP, GROUP), 1)).astype(F32).astype(BF16)
    return jnp.dot(hits.astype(BF16), tri, preferred_element_type=F32)


def targets_of(ids, copies):
    experts = copies.shape[1]
    total = jnp.zeros(ids.shape, F32)
    for e in range(experts):
        total = total + jnp.where(ids == float(e), copies[:, e : e + 1], 0.0)
    return total


def collect_kernel(nep, nt, attn, w_out, residual, ids, copies, rows_out, load_out, send_sem, recv_sem):
    ep, tp = lax.axis_index("ep"), lax.axis_index("tp")
    ny = nep // 2
    y, core = ep // 2, lax.rem(ep, 2)
    mate = 2 * y + (1 - core)

    def peer(k):
        return 2 * lax.rem(y + k, ny) + core

    barrier = pltpu.get_barrier_semaphore()
    for k in range(1, ny):
        pl.semaphore_signal(barrier, inc=1, device_id={"ep": peer(k), "tp": tp}, device_id_type=MESH)
    pl.semaphore_signal(barrier, inc=1, device_id={"ep": mate, "tp": tp}, device_id_type=MESH)

    product = jnp.dot(attn[...], w_out[...], preferred_element_type=F32).astype(BF16).astype(F32)
    pair = residual[:, pl.ds(pl.multiple_of((tp // 2) * 128, 128), 128)].astype(F32)
    left = left_half((GROUP, 128))
    odd = lax.rem(tp, 2) == 1
    pair = jnp.where(odd, swap(pair), pair)
    carried = pair + jnp.concatenate([product, product], axis=1)
    packed = jnp.where(left[:CAP], carried[:CAP], swap(carried[CAP:]))
    rows_out[ep, 0:CAP, :] = packed.astype(BF16)
    names = ids[...].astype(F32)
    rows_out[ep, CAP : CAP + 16, :] = jnp.concatenate(
        [names, jnp.zeros((14, GROUP), F32)], axis=0
    ).astype(BF16)

    pl.semaphore_wait(barrier, ny)

    def copy(slot, where, index):
        return pltpu.make_async_remote_copy(
            src_ref=rows_out.at[slot],
            dst_ref=rows_out.at[slot],
            send_sem=send_sem.at[index],
            recv_sem=recv_sem.at[index],
            device_id={"ep": where, "tp": tp},
            device_id_type=MESH,
        )

    order = sorted(range(1, ny), key=lambda k: (-min(k, ny - k), k))
    own = [copy(ep, mate, 0)] + [copy(ep, peer(k), k) for k in order]
    for c in own:
        c.start()
    passed = []
    for k in reversed(order):
        came = 2 * lax.rem(y + ny - k, ny) + core
        copy(came, peer(k), k).wait_recv()
        relay = copy(came, mate, ny + k)
        relay.start()
        passed.append(relay)
    copy(2 * y + 1 - core, mate, 0).wait_recv()
    for k in reversed(order):
        copy(2 * lax.rem(y + ny - k, ny) + 1 - core, mate, ny + k).wait_recv()
    for c in own + passed:
        c.wait_send()

    table = rows_out[:, CAP : CAP + 16, :].astype(F32)
    first = targets_of(table[:, 0, :], copies[...])
    second = targets_of(table[:, 1, :], copies[...])
    most = jnp.zeros((1, 1), F32)
    for q in range(ny):
        lo, hi = float(2 * q), float(2 * q + 1)
        hits = ((first >= lo) & (first <= hi)).astype(F32) + ((second >= lo) & (second <= hi)).astype(F32)
        most = jnp.maximum(most, jnp.sum(jnp.sum(hits, axis=1, keepdims=True), axis=0, keepdims=True))
    load_out[...] = jnp.broadcast_to(most, (8, 128)).astype(jnp.int32)


def expert_kernel(
    nep, nt, width, half_rows,
    rows, copies, logits, gain_in, gain_out, w_gate, w_up, w_down,
    layer_out, next_out,
    pick, flat_l, flat_r, got, full, gates, ups, downs, hid, share, landed, fin, ret_pick, ret_l, ret_r,
    back, slots, outgoing, incoming, whole,
    gs_send, gs_recv, rs_send, rs_recv, w_local, w_send, w_recv, x_send, x_recv, e_send, e_recv, f_send, f_recv,
):
    ep, tp = lax.axis_index("ep"), lax.axis_index("tp")
    nx = NX if nt > 8 else 2
    nz = nt // nx
    ny = nep // 2
    y, core = ep // 2, lax.rem(ep, 2)
    mate = 2 * y + (1 - core)
    z, x = tp // nx, lax.rem(tp, nx)
    hp = half_rows // 2
    a = (hp * 2 // 5) // 32 * 32
    parts = {"a": (0, a), "b": (a, hp - a)}
    own_rows = GROUP // nt

    def device(where_ep, where_tp):
        return {"ep": where_ep, "tp": where_tp}

    barrier = pltpu.get_barrier_semaphore()
    for k in range(1, nt):
        pl.semaphore_signal(
            barrier, inc=1, device_id=device(ep, lax.rem(tp + k, nt)), device_id_type=MESH
        )
    for k in range(1, nep):
        pl.semaphore_signal(
            barrier, inc=1, device_id=device(lax.rem(ep + k, nep), tp), device_id_type=MESH
        )

    own_weights = [
        pltpu.make_async_copy(src.at[0], dst.at[0], w_local.at[i])
        for i, (src, dst) in enumerate(((w_gate, gates), (w_up, ups), (w_down, downs)))
    ]
    for c in own_weights:
        c.start()

    table = rows[:, CAP : CAP + 16, :].astype(F32)
    aims = [targets_of(table[:, k, :], copies[...]) for k in range(2)]
    low = (2 * y).astype(F32)
    hits = [
        ((aims[0] == low + c).astype(F32) + (aims[1] == low + c).astype(F32)) for c in (0.0, 1.0)
    ]
    before = [rank_before(h) for h in hits]
    totals = [jnp.sum(h, axis=1, keepdims=True) for h in hits]
    lower = (iota((nep, nep), 1) < iota((nep, nep), 0)).astype(F32).astype(BF16)
    offsets = [
        jnp.dot(lower, jnp.broadcast_to(t, (nep, 128)).astype(BF16), preferred_element_type=F32)
        for t in totals
    ]
    count_low = jnp.sum(totals[0], axis=0, keepdims=True)
    starts = [offsets[0], offsets[1] + count_low]
    places = [starts[c] + before[c] for c in range(2)]
    spots = [
        jnp.where(
            aims[k] == low, places[0], jnp.where(aims[k] == low + 1.0, places[1], -1.0)
        )
        for k in range(2)
    ]

    left64 = left_half((CAP, 128))
    for s in range(nep):
        packed = rows[s, 0:CAP, :].astype(F32)
        other = swap(packed)
        at = s * GROUP
        flat_l[at : at + CAP, :] = jnp.where(left64, packed, 0.0).astype(BF16)
        flat_l[at + CAP : at + GROUP, :] = jnp.where(left64, other, 0.0).astype(BF16)
        flat_r[at : at + CAP, :] = jnp.where(left64, 0.0, other).astype(BF16)
        flat_r[at + CAP : at + GROUP, :] = jnp.where(left64, 0.0, packed).astype(BF16)
    base = (core * half_rows).astype(F32)
    piece = jnp.zeros((hp, 128), F32)
    for q, flat in enumerate((flat_l, flat_r)):
        line = iota((hp, 128), 0).astype(F32) + base + float(q * hp)
        for s in range(nep):
            hit = (spots[0][s : s + 1, :] == line) | (spots[1][s : s + 1, :] == line)
            pick[:, s * GROUP : (s + 1) * GROUP] = jnp.where(hit, 1.0, 0.0).astype(BF16)
        piece = piece + jnp.dot(pick[...], flat[...], preferred_element_type=F32)
    got[0, 0, :, :] = piece.astype(BF16)

    pl.semaphore_wait(barrier, nt - 1 + nep - 1)

    def move(src, dst, send, recv, where):
        return pltpu.make_async_remote_copy(
            src_ref=src, dst_ref=dst, send_sem=send, recv_sem=recv, device_id=where, device_id_type=MESH
        )

    mate_weights = [
        move(src.at[0], dst.at[1], w_send.at[i], w_recv.at[i], device(mate, tp))
        for i, (src, dst) in enumerate(((w_gate, gates), (w_up, ups), (w_down, downs)))
    ]

    def neighbour(axis, sign):
        if axis == "z":
            return device(ep, lax.rem(z + sign + nz, nz) * nx + x)
        return device(ep, z * nx + lax.rem(x + sign + nx, nx))

    count = {"z": nz, "x": nx}

    def slot_of(axis, offset, other):
        return (offset % nz, other) if axis == "z" else (other, offset % nx)

    keys, ops = gather_plan(nz, nx, parts)

    def gather_copy(key):
        part, axis, sign, dist, other = key
        start, size = row_range(parts, part, sign, dist, count[axis])
        src = slot_of(axis, sign * (dist - 1), other)
        dst = slot_of(axis, sign * dist, other)
        i = keys.index(key)
        return move(
            got.at[src[0], src[1], pl.ds(start, size), :],
            got.at[dst[0], dst[1], pl.ds(start, size), :],
            gs_send.at[i], gs_recv.at[i], neighbour(axis, sign),
        )

    sent = []
    for c in mate_weights:
        c.start()
        sent.append(c)
    for kind, key in ops:
        c = gather_copy(key)
        if kind == "start":
            c.start()
            sent.append(c)
        else:
            c.wait_recv()

    left = left_half((hp, 128))

    def join(i, carry):
        t0, t1 = 2 * i, 2 * i + 1
        p0, p1 = [
            got[lax.rem(z - t // nx + nz, nz), lax.rem(x - lax.rem(t, nx) + nx, nx)].astype(F32)
            for t in (t0, t1)
        ]
        lanes = pl.ds(pl.multiple_of(i * 128, 128), 128)
        full[0:hp, lanes] = jnp.where(left, p0, swap(p1)).astype(BF16)
        full[hp : 2 * hp, lanes] = jnp.where(left, swap(p0), p1).astype(BF16)
        return carry

    lax.fori_loop(0, nt // 2, join, 0)
    for c in own_weights:
        c.wait()
    for c in mate_weights:
        c.wait_recv()

    tile = 128
    count_own = jnp.broadcast_to(count_low, (tile, 1))
    core_f = core.astype(F32)

    def experts(i, carry):
        at = pl.ds(pl.multiple_of(i * tile, tile), tile)
        value = full[at, :].astype(F32)
        scale = lax.rsqrt(jnp.sum(value * value, axis=1, keepdims=True) * (1.0 / width) + 1e-06)
        normed = (value * scale * gain_in[...]).astype(BF16)
        spot = iota((tile, 1), 0).astype(F32) + base + (i * tile).astype(F32)
        in_low = (spot < count_own).astype(F32)
        mine = in_low * (1.0 - core_f) + (1.0 - in_low) * core_f
        for w, keep in ((0, mine), (1, 1.0 - mine)):
            gate = jnp.dot(normed, gates[w], preferred_element_type=F32)
            up = jnp.dot(normed, ups[w], preferred_element_type=F32)
            value_h = gate / (1.0 + jnp.exp(-gate)) * up
            hid[w, at, :] = jnp.where(keep > 0.5, value_h, 0.0).astype(BF16)
        return carry

    lax.fori_loop(0, half_rows // tile, experts, 0)

    rs_keys, rs_ops, far = reduce_plan(nz, nx, parts, 0.4)
    land_at, total = {}, 0
    for key in rs_keys:
        size = row_range(parts, key[0], key[2], key[3], count[key[1]])[1]
        land_at[key] = (total, size)
        total += size

    def reduce_copy(key):
        part, axis, sign, dist, other = key
        start, size = row_range(parts, part, sign, dist, count[axis])
        src = slot_of(axis, sign * dist, other)
        i = rs_keys.index(key)
        return move(
            share.at[src[0], src[1], pl.ds(start, size), :],
            landed.at[pl.ds(land_at[key][0], size), :],
            rs_send.at[i], rs_recv.at[i], neighbour(axis, sign),
        )

    def chunk(dz):
        zt = lax.rem(z + dz, nz)
        lanes = pl.ds(pl.multiple_of(zt * (nx * COLS), 128), nx * COLS)
        wd = [downs[w, :, lanes] for w in range(2)]
        sides = []
        for q in range(2):
            at = slice(q * hp, (q + 1) * hp)
            sides.append(
                jnp.dot(hid[0, at, :], wd[0], preferred_element_type=F32)
                + jnp.dot(hid[1, at, :], wd[1], preferred_element_type=F32)
            )
        for i in range(nx // 2):
            top, low_side = [v[:, i * 128 : (i + 1) * 128] for v in sides]
            d0 = lax.rem(2 * i - x + nx, nx)
            d1 = lax.rem(2 * i + 1 - x + nx, nx)
            share[dz, d0] = jnp.where(left, top, swap(low_side)).astype(BF16)
            share[dz, d1] = jnp.where(left, swap(top), low_side).astype(BF16)

    for kind, key in rs_ops:
        if kind == "chunk":
            chunk(key)
            continue
        c = reduce_copy(key)
        if kind == "start":
            c.start()
            sent.append(c)
        else:
            c.wait_recv()
            part, axis, sign, dist, other = key
            start, size = row_range(parts, part, sign, dist, count[axis])
            at = slot_of(axis, sign * (dist - 1), other)
            here = pl.ds(start, size)
            there = pl.ds(land_at[key][0], size)
            share[at[0], at[1], here, :] = (
                share[at[0], at[1], here, :].astype(F32) + landed[there, :].astype(F32)
            ).astype(BF16)

    swap_copy = move(share.at[0, 0], fin, x_send.at[0], x_recv.at[0], device(mate, tp))
    swap_copy.start()
    sent.append(swap_copy)
    start_own = jnp.where(core == 0, starts[0], starts[1])
    joint = 2 * half_rows
    lead = (iota((CAP // 2, joint), 1) - iota((CAP // 2, joint), 0)).astype(F32)
    for q in range(2):
        for s in range(nep):
            first_spot = start_own[s : s + 1, 0:1] + float(q * (CAP // 2))
            at = s * (CAP // 2)
            ret_pick[q, at : at + CAP // 2, :] = jnp.where(lead == first_spot, 1.0, 0.0).astype(BF16)
    swap_copy.wait_recv()
    here_v = share[0, 0].astype(F32)
    there_v = fin[...].astype(F32)
    zero_core = core == 0
    for h in range(2):
        v = jnp.where(zero_core, here_v, there_v) if h == 0 else jnp.where(zero_core, there_v, here_v)
        w = swap(v)
        at = h * half_rows
        ret_l[at : at + hp, :] = jnp.where(left, v, 0.0).astype(BF16)
        ret_l[at + hp : at + 2 * hp, :] = jnp.where(left, w, 0.0).astype(BF16)
        ret_r[at : at + hp, :] = jnp.where(left, 0.0, w).astype(BF16)
        ret_r[at + hp : at + 2 * hp, :] = jnp.where(left, 0.0, v).astype(BF16)
    blocks = jnp.dot(ret_pick[0], ret_l[...], preferred_element_type=F32)
    blocks = blocks + jnp.dot(ret_pick[1], ret_r[...], preferred_element_type=F32)
    back[...] = blocks.astype(BF16).reshape(nep, CAP // 2, 128)

    def return_copy(k):
        to = lax.rem(ep + k, nep)
        return move(back.at[to], slots.at[ep], e_send.at[k], e_recv.at[k], device(to, tp))

    returns = [return_copy(k) for k in range(1, nep)]
    for c in returns:
        c.start()
        sent.append(c)
    slots[ep] = back[ep]

    own_ids = rows[ep, CAP : CAP + 16, :].astype(F32)
    experts_all = copies.shape[1]
    which = iota((experts_all, GROUP), 0).astype(F32)
    named = [jnp.broadcast_to(own_ids[k : k + 1, :], (experts_all, GROUP)) == which for k in range(2)]
    own_before = rank_before(named[0].astype(F32) + named[1].astype(F32))
    score = logits[...]
    chosen = [jnp.sum(jnp.where(m, score, 0.0), axis=0, keepdims=True) for m in named]
    ranks = [jnp.sum(jnp.where(m, own_before, 0.0), axis=0, keepdims=True) for m in named]
    own_copies = copies[pl.ds(ep, 1), :]
    own_aims = [
        sum(
            jnp.where(own_ids[k : k + 1, :] == float(e), own_copies[:, e : e + 1], 0.0)
            for e in range(experts_all)
        )
        for k in range(2)
    ]
    half_cap = float(CAP // 2)
    places_own = [
        jnp.where(r >= half_cap, float(nep) * half_cap - half_cap, 0.0) + t * half_cap + r
        for r, t in zip(ranks, own_aims)
    ]
    shares = [
        1.0 / (1.0 + jnp.exp(chosen[1] - chosen[0])),
        1.0 / (1.0 + jnp.exp(chosen[0] - chosen[1])),
    ]
    columns = jnp.concatenate(places_own + shares + [jnp.zeros((4, GROUP), F32)], axis=0).T
    lane = iota((GROUP, nep * CAP), 1).astype(F32)
    takes = [jnp.where(lane == columns[:, k : k + 1], 1.0, 0.0).astype(BF16) for k in range(2)]

    for k in range(1, nep):
        came = lax.rem(ep + nep - k, nep)
        move(back.at[ep], slots.at[came], e_send.at[k], e_recv.at[k], device(ep, tp)).wait_recv()
    arrived = slots[...].reshape(nep * CAP // 2, 128).astype(F32)
    left_slots = left_half(arrived.shape)
    stacked = jnp.concatenate(
        [jnp.where(left_slots, arrived, 0.0), jnp.where(left_slots, swap(arrived), 0.0)], axis=0
    ).astype(BF16)
    mixture = columns[:, 2:3] * jnp.dot(takes[0], stacked, preferred_element_type=F32)
    mixture = mixture + columns[:, 3:4] * jnp.dot(takes[1], stacked, preferred_element_type=F32)
    own_packed = rows[ep, 0:CAP, :].astype(F32)
    carried = jnp.concatenate([own_packed, swap(own_packed)], axis=0)
    layer = carried + mixture
    for t in range(nt):
        outgoing[t] = layer[t * own_rows : (t + 1) * own_rows, :].astype(BF16)

    def owner_copy(k):
        to = lax.rem(tp + k, nt)
        return move(outgoing.at[to], incoming.at[tp], f_send.at[k], f_recv.at[k], device(ep, to))

    owners = [owner_copy(k) for k in range(1, nt)]
    for c in owners:
        c.start()
        sent.append(c)
    incoming[tp] = outgoing[tp]
    for k in range(1, nt):
        came = lax.rem(tp + nt - k, nt)
        move(outgoing.at[tp], incoming.at[came], f_send.at[k], f_recv.at[k], device(ep, tp)).wait_recv()
    left_own = left_half((own_rows, 128))
    for i in range(nt // 2):
        v0, v1 = incoming[2 * i].astype(F32), incoming[2 * i + 1].astype(F32)
        whole[:, i * 128 : (i + 1) * 128] = jnp.where(left_own, v0, swap(v1))
    value = whole[...]
    layer_out[...] = value.astype(BF16)
    scale = lax.rsqrt(jnp.sum(value * value, axis=1, keepdims=True) * (1.0 / width) + 1e-06)
    next_out[...] = (value * scale * gain_out[...]).astype(BF16)
    for c in sent:
        c.wait_send()


def collect(attn_out, w_out, residual_in, ids, copies, nep, nt):
    vmem = pl.BlockSpec(memory_space=pltpu.VMEM)
    ny = nep // 2
    return pl.pallas_call(
        functools.partial(collect_kernel, nep, nt),
        out_shape=(
            jax.ShapeDtypeStruct((nep, CAP + 16, 128), BF16),
            jax.ShapeDtypeStruct((8, 128), jnp.int32),
        ),
        in_specs=[vmem] * 5,
        out_specs=(vmem, vmem),
        scratch_shapes=[pltpu.SemaphoreType.DMA((2 * ny,)), pltpu.SemaphoreType.DMA((2 * ny,))],
        compiler_params=pltpu.CompilerParams(collective_id=0, has_side_effects=True),
        name="collect",
    )(attn_out, w_out, residual_in, ids, copies)


def experts_call(half_rows, which, nep, nt, rows, copies, logits, gain_in, gain_out, w_gate, w_up, w_down):
    vmem = pl.BlockSpec(memory_space=pltpu.VMEM)
    hbm = pl.BlockSpec(memory_space=pl.ANY)
    width, inner = w_gate.shape[1], w_gate.shape[2]
    nx = NX if nt > 8 else 2
    nz = nt // nx
    hp = half_rows // 2
    a = (hp * 2 // 5) // 32 * 32
    parts = {"a": (0, a), "b": (a, hp - a)}
    own_rows = GROUP // nt
    keys = gather_plan(nz, nx, parts)[0]
    rs_keys = reduce_plan(nz, nx, parts, 0.4)[0]
    land = sum(row_range(parts, k[0], k[2], k[3], {"z": nz, "x": nx}[k[1]])[1] for k in rs_keys)
    dma = pltpu.SemaphoreType.DMA
    out = jax.ShapeDtypeStruct((own_rows, width), BF16)
    return pl.pallas_call(
        functools.partial(expert_kernel, nep, nt, width, half_rows),
        out_shape=(out, out),
        in_specs=[vmem] * 5 + [hbm] * 3,
        out_specs=(vmem, vmem),
        scratch_shapes=[
            pltpu.VMEM((hp, nep * GROUP), BF16),
            pltpu.VMEM((nep * GROUP, 128), BF16),
            pltpu.VMEM((nep * GROUP, 128), BF16),
            pltpu.VMEM((nz, nx, hp, 128), BF16),
            pltpu.VMEM((half_rows, width), BF16),
            pltpu.VMEM((2, width, inner), BF16),
            pltpu.VMEM((2, width, inner), BF16),
            pltpu.VMEM((2, inner, width), BF16),
            pltpu.VMEM((2, half_rows, inner), BF16),
            pltpu.VMEM((nz, nx, hp, 128), BF16),
            pltpu.VMEM((land, 128), BF16),
            pltpu.VMEM((hp, 128), BF16),
            pltpu.VMEM((2, nep * CAP // 2, 2 * half_rows), BF16),
            pltpu.VMEM((2 * half_rows, 128), BF16),
            pltpu.VMEM((2 * half_rows, 128), BF16),
            pltpu.VMEM((nep, CAP // 2, 128), BF16),
            pltpu.VMEM((nep, CAP // 2, 128), BF16),
            pltpu.VMEM((nt, own_rows, 128), BF16),
            pltpu.VMEM((nt, own_rows, 128), BF16),
            pltpu.VMEM((own_rows, width), F32),
            dma((len(keys),)), dma((len(keys),)),
            dma((len(rs_keys),)), dma((len(rs_keys),)),
            dma((3,)), dma((3,)), dma((3,)),
            dma((1,)), dma((1,)),
            dma((nep,)), dma((nep,)),
            dma((nt,)), dma((nt,)),
        ],
        compiler_params=pltpu.CompilerParams(
            collective_id=which, has_side_effects=True, vmem_limit_bytes=60 * 2**20
        ),
        name="experts_%d" % half_rows,
    )(rows, copies, logits, gain_in, gain_out, w_gate, w_up, w_down)


def per_device(sizes, attn_out, residual_in, w_out, gain_in, router_logits, expert_ids, copy_of, w_gate, w_up, w_down, gain_out):
    nt, nep = lax.axis_size("tp"), lax.axis_size("ep")
    copies = copy_of.astype(F32)
    rows, load = collect(attn_out, w_out, residual_in, expert_ids.T, copies, nep, nt)
    operands = (
        rows, copies, router_logits.T, gain_in[None, :], gain_out[None, :], w_gate, w_up, w_down
    )
    branches = [
        functools.partial(experts_call, size, i + 1, nep, nt) for i, size in enumerate(sizes)
    ]
    if len(branches) == 1:
        return branches[0](*operands)
    most = load[0, 0]
    choice = sum((most > 2 * size).astype(jnp.int32) for size in sizes[:-1])
    return lax.switch(choice, branches, *operands)


def solution(mesh, sizes=(512, 640, 1024)):
    return jax.shard_map(
        functools.partial(per_device, sizes),
        mesh=mesh,
        in_specs=(
            P("ep", None),
            P("ep", None),
            P(None, "tp"),
            P(),
            P("ep", None),
            P("ep", None),
            P(),
            P("ep", None, "tp"),
            P("ep", None, "tp"),
            P("ep", "tp", None),
            P(),
        ),
        out_specs=(P(("ep", "tp"), None), P(("ep", "tp"), None)),
        check_vma=False,
    )
```

```python
import functools
import heapq

import jax
import jax.numpy as jnp
from jax import lax
from jax.experimental import pallas as pl
from jax.experimental.pallas import tpu as pltpu
from jax.sharding import PartitionSpec as P

MESH = pl.DeviceIdType.MESH
F32 = jnp.float32
BF16 = jnp.bfloat16
NX = 4
COLS = 64
GROUP = 128
CAP = 64
SIGNS = (1, -1)


def row_range(parts, part, sign, dist, count):
    start, size = parts[part]
    if 2 * dist == count:
        half = size // 2
        return (start, half) if sign > 0 else (start + half, half)
    return (start, size)


def split_rows(half, pieces):
    units, out, at, taken = half // 32, [], 0, 0
    for i in range(pieces):
        size = (units * (i + 1) // pieces) * 32 - at
        first = int(0.41 * (at + size) / 32 + 0.5) * 32 - taken
        first = min(max(first, 32), size - 32)
        out.append((at, first, size - first))
        at, taken = at + size, taken + first
    return out


def part_of(pieces, u):
    start, first, second = pieces[u]
    return {"a": (start, first), "b": (start + first, second)}


def gather_sends(nz, nx, pieces, u):
    count, parts, sends = {"z": nz, "x": nx}, part_of(pieces, u), {}
    for part, (first, second) in (("a", ("x", "z")), ("b", ("z", "x"))):
        for axis in (first, second):
            n = count[axis]
            for other in range(1 if axis == first else count[first]):
                for dist in range(1, n // 2 + 1):
                    for sign in SIGNS:
                        need = set()
                        if dist > 1:
                            need.add(("g", u, part, axis, sign, dist - 1, other))
                        elif axis == second and other:
                            m = count[first]
                            if 2 * other <= m:
                                need.add(("g", u, part, first, 1, other, 0))
                            if 2 * other >= m:
                                need.add(("g", u, part, first, -1, m - other, 0))
                        size = row_range(parts, part, sign, dist, n)[1]
                        sends[("g", u, part, axis, sign, dist, other)] = ((axis, sign), size, need)
    return sends


def reduce_sends(nz, nx, pieces, u):
    count, parts, sends = {"z": nz, "x": nx}, part_of(pieces, u), {}
    for part, (first, second) in (("a", ("z", "x")), ("b", ("x", "z"))):
        for axis in (first, second):
            n = count[axis]
            for other in range(count[second] if axis == first else 1):
                for dist in range(n // 2, 0, -1):
                    for sign in SIGNS:
                        offset = (sign * dist) % n
                        need = {("c", u, offset if axis == "z" else other)}
                        if 2 * dist < n:
                            need.add(("r", u, part, axis, sign, dist + 1, other))
                        if axis == second:
                            for way in SIGNS:
                                need.add(("r", u, part, first, way, 1, offset))
                        size = row_range(parts, part, sign, dist, n)[1]
                        sends[("r", u, part, axis, sign, dist, other)] = ((axis, sign), size, need)
    return sends


def schedule(nz, nx, pieces):
    rate, latency = 181.0, 1.7
    sends, tasks, landing, total = {}, {}, {}, 0
    far = sorted(range(nz), key=lambda d: (-min(d, nz - d), d))
    for u, (_, first, second) in enumerate(pieces):
        gathers = gather_sends(nz, nx, pieces, u)
        reduces = reduce_sends(nz, nx, pieces, u)
        sends.update(gathers)
        sends.update(reduces)
        rows = first + second
        tasks[("x", u)] = (rows * 0.011, set(gathers))
        before = ("x", u)
        for dz in far:
            tasks[("c", u, dz)] = (rows * 0.0007, {before})
            before = ("c", u, dz)
        for key, value in reduces.items():
            landing[key] = (total, value[1])
            total += value[1]
    done, free, ops, arrivals = set(), {}, [], []
    waiting, later, now = dict(sends), dict(tasks), 0.0

    def release():
        for key in [k for k, v in waiting.items() if v[2] <= done]:
            link, size, _ = waiting.pop(key)
            free[link] = max(now, free.get(link, 0.0)) + size / rate
            ops.append(("start", key))
            heapq.heappush(arrivals, (free[link] + latency, len(ops), key))

    release()
    while arrivals or later:
        if arrivals and arrivals[0][0] <= now:
            key = heapq.heappop(arrivals)[2]
            ops.append(("wait", key))
            now += 0.05 + (sends[key][1] * 0.0006 if key[0] == "r" else 0.0)
            done.add(key)
            release()
            continue
        able = [k for k, v in later.items() if v[1] <= done]
        if able:
            now += later.pop(able[0])[0]
            ops.append(("task", able[0]))
            done.add(able[0])
            release()
            continue
        now = max(now, arrivals[0][0])
    assert not waiting
    return {key: i for i, key in enumerate(sends)}, ops, landing, total


def iota(shape, dim):
    return lax.broadcasted_iota(jnp.int32, shape, dim)


def left_half(shape):
    return iota(shape, len(shape) - 1) < COLS


def swap(value):
    return pltpu.roll(value, COLS, value.ndim - 1)


def rank_before(hits):
    tri = (iota((GROUP, GROUP), 0) < iota((GROUP, GROUP), 1)).astype(F32).astype(BF16)
    return jnp.dot(hits.astype(BF16), tri, preferred_element_type=F32)


def targets_of(ids, copies):
    experts = copies.shape[1]
    total = jnp.zeros(ids.shape, F32)
    for e in range(experts):
        total = total + jnp.where(ids == float(e), copies[:, e : e + 1], 0.0)
    return total


def contract(lhs, rhs):
    return lax.dot_general(lhs, rhs, (((1,), (1,)), ((), ())), preferred_element_type=F32)


def collect_kernel(
    nep, nt, sizes,
    attn, w_out, residual, ids, copies,
    rows_out, names_out, aims_out, choice,
    columns, by_group, local_sem, send_sem, recv_sem,
):
    ep, tp = lax.axis_index("ep"), lax.axis_index("tp")
    ny = nep // 2
    y, core = ep // 2, lax.rem(ep, 2)

    barrier = pltpu.get_barrier_semaphore()
    for k in range(1, nep):
        pl.semaphore_signal(
            barrier, inc=1, device_id={"ep": lax.rem(ep + k, nep), "tp": tp}, device_id_type=MESH
        )
    fetch = pltpu.make_async_copy(
        residual.at[:, pl.ds(pl.multiple_of((tp // 2) * 128, 128), 128)], columns, local_sem.at[0]
    )
    fetch.start()
    names = ids[...].astype(F32)
    names_out[core, y] = jnp.concatenate([names, jnp.zeros((14, GROUP), F32)], axis=0).astype(BF16)
    experts = copies.shape[0]
    padded = jnp.concatenate([copies[...].astype(F32), jnp.zeros((experts, 128 - nep), F32)], axis=1)
    if experts < 8:
        padded = jnp.concatenate([padded, jnp.zeros((8 - experts, 128), F32)], axis=0)
    by_group[...] = padded.T
    product = contract(attn[...], w_out[...]).astype(BF16).astype(F32)
    fetch.wait()
    pair = columns[...].astype(F32)
    left = left_half((CAP, 128))
    pair = jnp.where(lax.rem(tp, 2) == 1, swap(pair), pair)
    carried = pair + jnp.concatenate([product, product], axis=1)
    packed = jnp.where(left, carried[:CAP], swap(carried[CAP:]))
    rows_out[y] = packed.astype(BF16)

    pl.semaphore_wait(barrier, nep - 1)

    def send_names(k, parity, plane):
        return pltpu.make_async_remote_copy(
            src_ref=names_out.at[parity, plane],
            dst_ref=names_out.at[parity, plane],
            send_sem=send_sem.at[k],
            recv_sem=recv_sem.at[k],
            device_id={"ep": lax.rem(ep + k, nep), "tp": tp},
            device_id_type=MESH,
        )

    def send_rows(k, plane):
        return pltpu.make_async_remote_copy(
            src_ref=rows_out.at[plane],
            dst_ref=rows_out.at[plane],
            send_sem=send_sem.at[nep + k],
            recv_sem=recv_sem.at[nep + k],
            device_id={"ep": 2 * lax.rem(y + k, ny) + core, "tp": tp},
            device_id_type=MESH,
        )

    sent = [send_names(k, core, y) for k in sorted(range(1, nep), key=lambda k: -min(k, nep - k))]
    sent += [send_rows(k, y) for k in sorted(range(1, ny), key=lambda k: -min(k, ny - k))]
    for c in sent:
        c.start()
    for k in range(1, nep):
        came = lax.rem(ep + nep - k, nep)
        send_names(k, lax.rem(came, 2), came // 2).wait_recv()

    table = names_out[...].astype(F32)
    by_copy = [by_group[pl.ds(p, ny, stride=2), :] for p in range(2)]
    hits = [jnp.zeros((ny, GROUP), F32) for p in range(2)]
    most = jnp.zeros((1, 128), F32)
    lane = iota((ny, 128), 1)
    for p in range(2):
        aims = [targets_of(table[p, :, k, :], by_copy[p][:, :experts]) for k in range(2)]
        for k in range(2):
            aims_out[k, p] = aims[k]
        sums = jnp.zeros((ny, 128), F32)
        for q in range(ny):
            low, high = float(2 * q), float(2 * q + 1)
            hit = sum(((v >= low) & (v <= high)).astype(F32) for v in aims)
            sums = sums + jnp.where(lane == q, jnp.sum(hit, axis=1, keepdims=True), 0.0)
        most = jnp.maximum(most, jnp.sum(sums, axis=0, keepdims=True))
    largest = jnp.max(most).astype(jnp.int32)
    choice[0] = sum((largest > size).astype(jnp.int32) for size in sizes[:-1]) + 0 * largest

    for k in range(1, ny):
        send_rows(k, lax.rem(y + ny - k, ny)).wait_recv()
    for c in sent:
        c.wait_send()


def expert_kernel(
    nep, nt, width, size, count_pieces,
    rows, names, aims, logits, gain_in, gain_out, w_gate, w_up, w_down,
    layer_out, next_out,
    pick, flat_l, flat_r, spots, got, full, gates, ups, downs, hid, share, landed, ret_pick, ret_start,
    ret_l, ret_r, back, slots, outgoing, incoming, whole,
    t_send, t_recv, w_local, w_send, w_recv, e_send, e_recv, f_send, f_recv,
):
    ep, tp = lax.axis_index("ep"), lax.axis_index("tp")
    nx = NX if nt > 8 else 2
    nz = nt // nx
    ny = nep // 2
    y, core = ep // 2, lax.rem(ep, 2)
    mate = 2 * y + (1 - core)
    z, x = tp // nx, lax.rem(tp, nx)
    hp = size // 2
    pieces = split_rows(hp, count_pieces)
    own_rows = GROUP // nt
    count = {"z": nz, "x": nx}

    def neighbour(axis, sign):
        if axis == "z":
            return {"ep": ep, "tp": lax.rem(z + sign + nz, nz) * nx + x}
        return {"ep": ep, "tp": z * nx + lax.rem(x + sign + nx, nx)}

    def plane_peer(k):
        return {"ep": 2 * lax.rem(y + k, ny) + core, "tp": tp}

    partner = {"ep": mate, "tp": tp}
    friends = [neighbour(axis, sign) for axis in ("z", "x") for sign in SIGNS] + [partner]
    friends += [plane_peer(k) for k in range(1, ny)]
    barrier = pltpu.get_barrier_semaphore()
    for friend in friends:
        pl.semaphore_signal(barrier, inc=1, device_id=friend, device_id_type=MESH)

    def move(src, dst, send, recv, where):
        return pltpu.make_async_remote_copy(
            src_ref=src, dst_ref=dst, send_sem=send, recv_sem=recv, device_id=where, device_id_type=MESH
        )

    weights = ((w_gate, gates), (w_up, ups), (w_down, downs))
    own_weights = [
        pltpu.make_async_copy(src.at[0], dst.at[0], w_local.at[i]) for i, (src, dst) in enumerate(weights)
    ]
    for c in own_weights:
        c.start()

    low = (2 * y).astype(F32)
    aim = [aims[k, core] for k in range(2)]
    hits = [sum((v == low + c).astype(F32) for v in aim) for c in (0.0, 1.0)]
    totals = [jnp.sum(h, axis=1, keepdims=True) for h in hits]
    lower = (iota((ny, ny), 1) < iota((ny, ny), 0)).astype(F32).astype(BF16)
    offsets = [
        jnp.dot(lower, jnp.broadcast_to(t, (ny, 128)).astype(BF16), preferred_element_type=F32)
        for t in totals
    ]
    count_low = jnp.sum(totals[0], axis=0, keepdims=True)
    starts = [offsets[0], offsets[1] + count_low]
    places = [starts[c] + rank_before(hits[c]) for c in range(2)]
    for k in range(2):
        spots[k] = jnp.where(
            aim[k] == low, places[0], jnp.where(aim[k] == low + 1.0, places[1], -1.0)
        )
    for c in range(2):
        ret_start[c] = starts[c]

    left64 = left_half((CAP, 128))

    def flatten(g, carry):
        packed = rows[g].astype(F32)
        other = swap(packed)
        top = pl.ds(pl.multiple_of(g * GROUP, GROUP), CAP)
        bottom = pl.ds(pl.multiple_of(g * GROUP + CAP, CAP), CAP)
        flat_l[top, :] = jnp.where(left64, packed, 0.0).astype(BF16)
        flat_l[bottom, :] = jnp.where(left64, other, 0.0).astype(BF16)
        flat_r[top, :] = jnp.where(left64, 0.0, other).astype(BF16)
        flat_r[bottom, :] = jnp.where(left64, 0.0, packed).astype(BF16)
        return carry

    lax.fori_loop(0, ny, flatten, 0)

    def choose(q):
        line = iota((hp, 128), 0).astype(F32) + float(q * hp)

        def one(g, carry):
            hit = (spots[0, pl.ds(g, 1), :] == line) | (spots[1, pl.ds(g, 1), :] == line)
            lanes = pl.ds(pl.multiple_of(g * GROUP, GROUP), GROUP)
            pick[:, lanes] = jnp.where(hit, 1.0, 0.0).astype(BF16)
            return carry

        lax.fori_loop(0, ny, one, 0)
        return jnp.dot(pick[...], (flat_l, flat_r)[q][...], preferred_element_type=F32)

    got[0, 0] = choose(0).astype(BF16)
    got[0, 0] = (got[0, 0].astype(F32) + choose(1)).astype(BF16)

    pl.semaphore_wait(barrier, len(friends))

    mate_weights = [
        move(src.at[0], dst.at[1], w_send.at[i], w_recv.at[i], partner)
        for i, (src, dst) in enumerate(weights)
    ]

    def slot_of(axis, offset, other):
        return (offset % nz, other) if axis == "z" else (other, offset % nx)

    index, ops, landing, _ = schedule(nz, nx, pieces)

    def transfer(key):
        kind, u, part, axis, sign, dist, other = key
        start, many = row_range(part_of(pieces, u), part, sign, dist, count[axis])
        i = index[key]
        if kind == "g":
            src, dst = slot_of(axis, sign * (dist - 1), other), slot_of(axis, sign * dist, other)
            target = got.at[dst[0], dst[1], pl.ds(start, many), :]
            source = got.at[src[0], src[1], pl.ds(start, many), :]
        else:
            src = slot_of(axis, sign * dist, other)
            target = landed.at[pl.ds(landing[key][0], many), :]
            source = share.at[src[0], src[1], pl.ds(start, many), :]
        return move(source, target, t_send.at[i], t_recv.at[i], neighbour(axis, sign))

    def add_landed(key):
        _, u, part, axis, sign, dist, other = key
        start, many = row_range(part_of(pieces, u), part, sign, dist, count[axis])
        at = slot_of(axis, sign * (dist - 1), other)
        here, there = pl.ds(start, many), pl.ds(landing[key][0], many)
        share[at[0], at[1], here, :] = (
            share[at[0], at[1], here, :].astype(F32) + landed[there, :].astype(F32)
        ).astype(BF16)

    core_f = core.astype(F32)

    def experts(u):
        start, many = pieces[u][0], pieces[u][1] + pieces[u][2]
        at = 2 * start
        here = pl.ds(start, many)
        left = left_half((many, 128))

        def join(i, carry):
            p0, p1 = [
                got[
                    lax.rem(z - t // nx + nz, nz), lax.rem(x - lax.rem(t, nx) + nx, nx), here, :
                ].astype(F32)
                for t in (2 * i, 2 * i + 1)
            ]
            lanes = pl.ds(pl.multiple_of(i * 128, 128), 128)
            full[at : at + many, lanes] = jnp.where(left, p0, swap(p1)).astype(BF16)
            full[at + many : at + 2 * many, lanes] = jnp.where(left, swap(p0), p1).astype(BF16)
            return carry

        lax.fori_loop(0, nt // 2, join, 0)
        tile = next(t for t in (128, 96, 160, 64, 32) if many % t == 0)
        sides = many // tile

        def one(i, carry):
            span = pl.ds(pl.multiple_of(at + i * tile, 32), tile)
            value = full[span, :].astype(F32)
            scale = lax.rsqrt(jnp.sum(value * value, axis=1, keepdims=True) * (1.0 / width) + 1e-06)
            normed = (value * scale * gain_in[...]).astype(BF16)
            first = start + lax.rem(i, sides) * tile + (i // sides) * hp
            spot = (iota((tile, 1), 0) + first).astype(F32)
            in_low = (spot < jnp.broadcast_to(count_low, (tile, 1))).astype(F32)
            mine = in_low * (1.0 - core_f) + (1.0 - in_low) * core_f
            for w, keep in ((0, mine), (1, 1.0 - mine)):
                gate = contract(normed, gates[w])
                up = contract(normed, ups[w])
                value_h = gate / (1.0 + jnp.exp(-gate)) * up
                hid[w, span, :] = jnp.where(keep > 0.5, value_h, 0.0).astype(BF16)
            return carry

        lax.fori_loop(0, 2 * sides, one, 0)

    def down(u, dz):
        start, many = pieces[u][0], pieces[u][1] + pieces[u][2]
        left = left_half((many, 128))
        lanes = pl.ds(pl.multiple_of(lax.rem(z + dz, nz) * (nx * COLS), 128), nx * COLS)
        wd = [downs[w, :, lanes] for w in range(2)]
        sides = []
        for q in range(2):
            at = slice(2 * start + q * many, 2 * start + (q + 1) * many)
            sides.append(
                jnp.dot(hid[0, at, :], wd[0], preferred_element_type=F32)
                + jnp.dot(hid[1, at, :], wd[1], preferred_element_type=F32)
            )
        here = pl.ds(start, many)
        for i in range(nx // 2):
            top, bottom = [v[:, i * 128 : (i + 1) * 128] for v in sides]
            d0 = lax.rem(2 * i - x + nx, nx)
            d1 = lax.rem(2 * i + 1 - x + nx, nx)
            share[dz, d0, here, :] = jnp.where(left, top, swap(bottom)).astype(BF16)
            share[dz, d1, here, :] = jnp.where(left, swap(top), bottom).astype(BF16)

    sent = list(mate_weights)
    for c in mate_weights:
        c.start()
    have_weights = False
    for kind, key in ops:
        if kind == "task":
            if key[0] == "x":
                if not have_weights:
                    have_weights = True
                    for c in own_weights:
                        c.wait()
                    for c in mate_weights:
                        c.wait_recv()
                experts(key[1])
            else:
                down(key[1], key[2])
            continue
        c = transfer(key)
        if kind == "start":
            c.start()
            sent.append(c)
        else:
            c.wait_recv()
            if key[0] == "r":
                add_landed(key)

    left = left_half((hp, 128))
    half_cap = CAP // 2
    lead = (iota((half_cap, size), 1) - iota((half_cap, size), 0)).astype(F32)
    for q in range(2):
        for c in range(2):

            def mark(g, carry, q=q, c=c):
                first = ret_start[c, pl.ds(g, 1), 0:1] + float(q * half_cap)
                at = pl.ds(pl.multiple_of(g * CAP + c * half_cap, half_cap), half_cap)
                ret_pick[q, at, :] = jnp.where(lead == first, 1.0, 0.0).astype(BF16)
                return carry

            lax.fori_loop(0, ny, mark, 0)
    v = share[0, 0].astype(F32)
    w = swap(v)
    ret_l[0:hp, :] = jnp.where(left, v, 0.0).astype(BF16)
    ret_l[hp : 2 * hp, :] = jnp.where(left, w, 0.0).astype(BF16)
    ret_r[0:hp, :] = jnp.where(left, 0.0, w).astype(BF16)
    ret_r[hp : 2 * hp, :] = jnp.where(left, 0.0, v).astype(BF16)
    blocks = jnp.dot(ret_pick[0], ret_l[...], preferred_element_type=F32)
    blocks = blocks + jnp.dot(ret_pick[1], ret_r[...], preferred_element_type=F32)
    back[...] = blocks.astype(BF16).reshape(ny, CAP, 128)

    def return_copy(k, to, came):
        return move(back.at[to], slots.at[came], e_send.at[k], e_recv.at[k], plane_peer(k))

    returns = [
        return_copy(k, lax.rem(y + k, ny), y)
        for k in sorted(range(1, ny), key=lambda k: -min(k, ny - k))
    ]
    for c in returns:
        c.start()
        sent.append(c)
    slots[y] = back[y]

    own_ids = names[core, y].astype(F32)
    experts_all = logits.shape[0]
    which = iota((experts_all, GROUP), 0).astype(F32)
    named = [jnp.broadcast_to(own_ids[k : k + 1, :], (experts_all, GROUP)) == which for k in range(2)]
    own_before = rank_before(named[0].astype(F32) + named[1].astype(F32))
    score = logits[...]
    chosen = [jnp.sum(jnp.where(m, score, 0.0), axis=0, keepdims=True) for m in named]
    ranks = [jnp.sum(jnp.where(m, own_before, 0.0), axis=0, keepdims=True) for m in named]
    own_aims = [aims[k, core, pl.ds(y, 1), :] for k in range(2)]
    places_own = [
        jnp.where(r >= float(half_cap), float((nep - 1) * half_cap), 0.0) + t * float(half_cap) + r
        for r, t in zip(ranks, own_aims)
    ]
    shares = [
        1.0 / (1.0 + jnp.exp(chosen[1] - chosen[0])),
        1.0 / (1.0 + jnp.exp(chosen[0] - chosen[1])),
    ]
    table = jnp.concatenate(places_own + shares + [jnp.zeros((4, GROUP), F32)], axis=0).T
    lane = iota((GROUP, nep * CAP), 1).astype(F32)
    takes = [jnp.where(lane == table[:, k : k + 1], 1.0, 0.0).astype(BF16) for k in range(2)]

    for k in range(1, ny):
        return_copy(k, y, lax.rem(y + ny - k, ny)).wait_recv()
    arrived = slots[...].reshape(ny * CAP, 128).astype(F32)
    left_slots = left_half(arrived.shape)
    stacked = jnp.concatenate(
        [jnp.where(left_slots, arrived, 0.0), jnp.where(left_slots, swap(arrived), 0.0)], axis=0
    ).astype(BF16)
    mixture = table[:, 2:3] * jnp.dot(takes[0], stacked, preferred_element_type=F32)
    mixture = mixture + table[:, 3:4] * jnp.dot(takes[1], stacked, preferred_element_type=F32)
    own_packed = rows[y].astype(F32)
    layer = jnp.concatenate([own_packed, swap(own_packed)], axis=0) + mixture
    for t in range(nt):
        outgoing[t] = layer[t * own_rows : (t + 1) * own_rows, :].astype(BF16)

    def owner_copy(k, to, came):
        where = {"ep": ep, "tp": lax.rem(tp + k, nt)}
        return move(outgoing.at[to], incoming.at[came], f_send.at[k], f_recv.at[k], where)

    def hops(k):
        return min(k // nx, nz - k // nx) + min(k % nx, nx - k % nx)

    owners = [
        owner_copy(k, lax.rem(tp + k, nt), tp) for k in sorted(range(1, nt), key=lambda k: -hops(k))
    ]
    for c in owners:
        c.start()
        sent.append(c)
    incoming[tp] = outgoing[tp]
    for k in range(1, nt):
        owner_copy(k, tp, lax.rem(tp + nt - k, nt)).wait_recv()
    left_own = left_half((own_rows, 128))
    for i in range(nt // 2):
        v0, v1 = incoming[2 * i].astype(F32), incoming[2 * i + 1].astype(F32)
        whole[:, i * 128 : (i + 1) * 128] = jnp.where(left_own, v0, swap(v1))
    value = whole[...]
    layer_out[...] = value.astype(BF16)
    scale = lax.rsqrt(jnp.sum(value * value, axis=1, keepdims=True) * (1.0 / width) + 1e-06)
    next_out[...] = (value * scale * gain_out[...]).astype(BF16)
    for c in sent:
        c.wait_send()


def collect(attn_out, w_out, residual_in, ids, copies, nep, nt, sizes):
    vmem = pl.BlockSpec(memory_space=pltpu.VMEM)
    ny = nep // 2
    dma = pltpu.SemaphoreType.DMA
    return pl.pallas_call(
        functools.partial(collect_kernel, nep, nt, sizes),
        out_shape=(
            jax.ShapeDtypeStruct((ny, CAP, 128), BF16),
            jax.ShapeDtypeStruct((2, ny, 16, 128), BF16),
            jax.ShapeDtypeStruct((2, 2, ny, 128), F32),
            jax.ShapeDtypeStruct((1,), jnp.int32),
        ),
        in_specs=[vmem, vmem, pl.BlockSpec(memory_space=pl.ANY), vmem, vmem],
        out_specs=(vmem, vmem, vmem, pl.BlockSpec(memory_space=pltpu.SMEM)),
        scratch_shapes=[
            pltpu.VMEM((GROUP, 128), BF16),
            pltpu.VMEM((128, 8), F32),
            dma((1,)),
            dma((nep + ny,)),
            dma((nep + ny,)),
        ],
        compiler_params=pltpu.CompilerParams(collective_id=0, has_side_effects=True),
        name="collect",
    )(attn_out, w_out, residual_in, ids, copies)


def experts_call(size, which, pieces, nep, nt, rows, names, aims, logits, gain_in, gain_out, w_gate, w_up, w_down):
    vmem = pl.BlockSpec(memory_space=pltpu.VMEM)
    hbm = pl.BlockSpec(memory_space=pl.ANY)
    inner, width = w_gate.shape[1], w_gate.shape[2]
    nx = NX if nt > 8 else 2
    nz = nt // nx
    ny = nep // 2
    hp = size // 2
    own_rows = GROUP // nt
    index, _, _, land = schedule(nz, nx, split_rows(hp, pieces))
    dma = pltpu.SemaphoreType.DMA
    out = jax.ShapeDtypeStruct((own_rows, width), BF16)
    return pl.pallas_call(
        functools.partial(expert_kernel, nep, nt, width, size, pieces),
        out_shape=(out, out),
        in_specs=[vmem] * 6 + [hbm] * 3,
        out_specs=(vmem, vmem),
        scratch_shapes=[
            pltpu.VMEM((hp, ny * GROUP), BF16),
            pltpu.VMEM((ny * GROUP, 128), BF16),
            pltpu.VMEM((ny * GROUP, 128), BF16),
            pltpu.VMEM((2, ny, 128), F32),
            pltpu.VMEM((nz, nx, hp, 128), BF16),
            pltpu.VMEM((size, width), BF16),
            pltpu.VMEM((2, inner, width), BF16),
            pltpu.VMEM((2, inner, width), BF16),
            pltpu.VMEM((2, inner, width), BF16),
            pltpu.VMEM((2, size, inner), BF16),
            pltpu.VMEM((nz, nx, hp, 128), BF16),
            pltpu.VMEM((land, 128), BF16),
            pltpu.VMEM((2, ny * CAP, size), BF16),
            pltpu.VMEM((2, ny, 128), F32),
            pltpu.VMEM((size, 128), BF16),
            pltpu.VMEM((size, 128), BF16),
            pltpu.VMEM((ny, CAP, 128), BF16),
            pltpu.VMEM((ny, CAP, 128), BF16),
            pltpu.VMEM((nt, own_rows, 128), BF16),
            pltpu.VMEM((nt, own_rows, 128), BF16),
            pltpu.VMEM((own_rows, width), F32),
            dma((len(index),)), dma((len(index),)),
            dma((3,)), dma((3,)), dma((3,)),
            dma((ny,)), dma((ny,)),
            dma((nt,)), dma((nt,)),
        ],
        compiler_params=pltpu.CompilerParams(
            collective_id=which, has_side_effects=True, vmem_limit_bytes=60 * 2**20
        ),
        name="experts_%d" % size,
    )(rows, names, aims, logits, gain_in, gain_out, w_gate, w_up, w_down)


def per_device(sizes, attn_out, residual_in, w_out, gain_in, router_logits, expert_ids, copy_of, w_gate, w_up, w_down, gain_out):
    nt, nep = lax.axis_size("tp"), lax.axis_size("ep")
    rows, names, aims, choice = collect(
        attn_out, w_out.T, residual_in, expert_ids.T, copy_of.T, nep, nt, tuple(s for s, _ in sizes)
    )
    operands = (
        rows, names, aims, router_logits.T, gain_in[None, :], gain_out[None, :],
        jnp.swapaxes(w_gate, 1, 2), jnp.swapaxes(w_up, 1, 2), w_down,
    )
    branches = [
        functools.partial(experts_call, size, i + 1, pieces, nep, nt)
        for i, (size, pieces) in enumerate(sizes)
    ]
    if len(branches) == 1:
        return branches[0](*operands)
    return lax.switch(choice[0], branches, *operands)


def solution(mesh, sizes=((512, 1), (640, 1), (1024, 1))):
    return jax.shard_map(
        functools.partial(per_device, sizes),
        mesh=mesh,
        in_specs=(
            P("ep", None),
            P("ep", None),
            P(None, "tp"),
            P(),
            P("ep", None),
            P("ep", None),
            P(),
            P("ep", None, "tp"),
            P("ep", None, "tp"),
            P("ep", "tp", None),
            P(),
        ),
        out_specs=(P(("ep", "tp"), None), P(("ep", "tp"), None)),
        check_vma=False,
    )
```

```python
import functools
import heapq

import jax
import jax.numpy as jnp
from jax import lax
from jax.experimental import pallas as pl
from jax.experimental.pallas import tpu as pltpu
from jax.sharding import PartitionSpec as P

MESH = pl.DeviceIdType.MESH
F32 = jnp.float32
BF16 = jnp.bfloat16
NX = 4
COLS = 64
GROUP = 128
CAP = 64
SIGNS = (1, -1)


def row_range(rows, sign, dist, count):
    if 2 * dist == count:
        half = rows // 2
        return (0, half) if sign > 0 else (half, half)
    return (0, rows)


AXES = (("z", "x"), ("x", "z"))
NEXT = {1: 0, 2: 1, 3: 2, 4: 3}
PAIR = {1: 0, 2: 0, 3: 2, 4: 2}


def ring_of(axis, core, n, rows):
    if axis == "z":
        ring = PAIR if core == 0 and rows <= 256 else NEXT
    else:
        ring = PAIR if rows <= 320 else NEXT
    return {d: p for d, p in ring.items() if 2 * d <= n}


def steps_of(nz, nx, rows):
    found = set()
    for core in range(2):
        for axis, n in (("z", nz), ("x", nx)):
            for dist, near in ring_of(axis, core, n, rows).items():
                for sign in SIGNS:
                    found.add((axis, sign * (dist - near) % n))
    return sorted(found)


def gather_sends(nz, nx, rows, core):
    count, sends = {"z": nz, "x": nx}, {}
    first, second = AXES[core]
    for axis in (first, second):
        n = count[axis]
        ring = ring_of(axis, core, n, rows)
        for other in range(1 if axis == first else count[first]):
            for dist, near in ring.items():
                for sign in SIGNS:
                    need = set()
                    if near:
                        need.add(("g", axis, sign, near, other))
                    elif axis == second and other:
                        m = count[first]
                        if 2 * other <= m:
                            need.add(("g", first, 1, other, 0))
                        if 2 * other >= m:
                            need.add(("g", first, -1, m - other, 0))
                    size = row_range(rows, sign, dist, n)[1]
                    sends[("g", axis, sign, dist, other)] = ((axis, sign), size * (dist - near), need)
    return sends


def reduce_sends(nz, nx, rows, core):
    count, sends = {"z": nz, "x": nx}, {}
    second, first = AXES[core]
    for axis in (first, second):
        n = count[axis]
        ring = ring_of(axis, core, n, rows)
        for other in range(count[second] if axis == first else 1):
            for dist in sorted(ring, reverse=True):
                for sign in SIGNS:
                    offset = (sign * dist) % n
                    need = {("c", offset if axis == "z" else other)}
                    for further, near in ring.items():
                        if near == dist:
                            need.add(("r", axis, sign, further, other))
                    if axis == second:
                        for further, near in ring_of(first, core, count[first], rows).items():
                            if near == 0:
                                for way in SIGNS:
                                    need.add(("r", first, way, further, offset))
                    size = row_range(rows, sign, dist, n)[1]
                    sends[("r", axis, sign, dist, other)] = (
                        (axis, sign), size * (dist - ring[dist]), need
                    )
    return sends


def timeline(sends, tasks):
    rate, latency = 330.0, 1.7
    done, free, ops, arrivals = set(), {}, [], []
    waiting, later, now = dict(sends), dict(tasks), 0.0

    def release():
        for key in [k for k, v in waiting.items() if v[2] <= done]:
            link, size, _ = waiting.pop(key)
            free[link] = max(now, free.get(link, 0.0)) + size / rate
            ops.append(("start", key))
            heapq.heappush(arrivals, (free[link] + latency, len(ops), key))

    release()
    while arrivals or later:
        if arrivals and arrivals[0][0] <= now:
            key = heapq.heappop(arrivals)[2]
            ops.append(("wait", key))
            now += 0.05 + (sends[key][1] * 0.0006 if key[0] == "r" else 0.0)
            done.add(key)
            release()
            continue
        able = [k for k, v in later.items() if v[1] <= done]
        if able:
            now += later.pop(able[0])[0]
            ops.append(("task", able[0]))
            done.add(able[0])
            release()
            continue
        now = max(now, arrivals[0][0])
    assert not waiting
    return ops


def gather_plan(nz, nx, rows, core):
    sends = gather_sends(nz, nx, rows, core)
    return list(sends), timeline(sends, {})


def reduce_plan(nz, nx, rows, core):
    sends = reduce_sends(nz, nx, rows, core)
    tasks, before = {}, set()
    for dz in sorted(range(nz), key=lambda d: (-min(d, nz - d), d)):
        tasks[("c", dz)] = (rows * 0.0009, before)
        before = {("c", dz)}
    landing, total = {}, 0
    for key, value in sends.items():
        many = row_range(rows, key[2], key[3], nz if key[1] == "z" else nx)[1]
        landing[key] = (total, many)
        total += many
    return list(sends), timeline(sends, tasks), landing, total


def iota(shape, dim):
    return lax.broadcasted_iota(jnp.int32, shape, dim)


def left_half(shape):
    return iota(shape, len(shape) - 1) < COLS


def swap(value):
    return pltpu.roll(value, COLS, value.ndim - 1)


def rank_before(hits):
    tri = (iota((GROUP, GROUP), 0) < iota((GROUP, GROUP), 1)).astype(F32).astype(BF16)
    return jnp.dot(hits.astype(BF16), tri, preferred_element_type=F32)


def targets_of(ids, copies):
    experts = copies.shape[1]
    total = jnp.zeros(ids.shape, F32)
    for e in range(experts):
        total = total + jnp.where(ids == float(e), copies[:, e : e + 1], 0.0)
    return total


def contract(lhs, rhs):
    return lax.dot_general(lhs, rhs, (((1,), (1,)), ((), ())), preferred_element_type=F32)


def collect_kernel(
    nep, nt, sizes,
    attn, w_out, residual, ids, copies,
    rows_out, names_out, aims_out, choice,
    columns, by_group, local_sem, send_sem, recv_sem,
):
    ep, tp = lax.axis_index("ep"), lax.axis_index("tp")
    ny = nep // 2
    y, core = ep // 2, lax.rem(ep, 2)

    barrier = pltpu.get_barrier_semaphore()
    for k in range(1, nep):
        pl.semaphore_signal(
            barrier, inc=1, device_id={"ep": lax.rem(ep + k, nep), "tp": tp}, device_id_type=MESH
        )
    fetch = pltpu.make_async_copy(
        residual.at[:, pl.ds(pl.multiple_of((tp // 2) * 128, 128), 128)], columns, local_sem.at[0]
    )
    fetch.start()
    names = ids[...].astype(F32)
    names_out[core, y] = jnp.concatenate([names, jnp.zeros((14, GROUP), F32)], axis=0).astype(BF16)
    experts = copies.shape[0]
    padded = jnp.concatenate([copies[...].astype(F32), jnp.zeros((experts, 128 - nep), F32)], axis=1)
    if experts < 8:
        padded = jnp.concatenate([padded, jnp.zeros((8 - experts, 128), F32)], axis=0)
    by_group[...] = padded.T
    product = contract(attn[...], w_out[...]).astype(BF16).astype(F32)
    fetch.wait()
    pair = columns[...].astype(F32)
    left = left_half((CAP, 128))
    pair = jnp.where(lax.rem(tp, 2) == 1, swap(pair), pair)
    carried = pair + jnp.concatenate([product, product], axis=1)
    packed = jnp.where(left, carried[:CAP], swap(carried[CAP:]))
    rows_out[y] = packed.astype(BF16)

    pl.semaphore_wait(barrier, nep - 1)

    def send_names(k, parity, plane):
        return pltpu.make_async_remote_copy(
            src_ref=names_out.at[parity, plane],
            dst_ref=names_out.at[parity, plane],
            send_sem=send_sem.at[k],
            recv_sem=recv_sem.at[k],
            device_id={"ep": lax.rem(ep + k, nep), "tp": tp},
            device_id_type=MESH,
        )

    def send_rows(k, plane):
        return pltpu.make_async_remote_copy(
            src_ref=rows_out.at[plane],
            dst_ref=rows_out.at[plane],
            send_sem=send_sem.at[nep + k],
            recv_sem=recv_sem.at[nep + k],
            device_id={"ep": 2 * lax.rem(y + k, ny) + core, "tp": tp},
            device_id_type=MESH,
        )

    sent = [send_names(k, core, y) for k in sorted(range(1, nep), key=lambda k: -min(k, nep - k))]
    sent += [send_rows(k, y) for k in sorted(range(1, ny), key=lambda k: -min(k, ny - k))]
    for c in sent:
        c.start()
    for k in range(1, nep):
        came = lax.rem(ep + nep - k, nep)
        send_names(k, lax.rem(came, 2), came // 2).wait_recv()

    table = names_out[...].astype(F32)
    by_copy = [by_group[pl.ds(p, ny, stride=2), :] for p in range(2)]
    hits = [jnp.zeros((ny, GROUP), F32) for p in range(2)]
    most = jnp.zeros((1, 128), F32)
    lane = iota((ny, 128), 1)
    for p in range(2):
        aims = [targets_of(table[p, :, k, :], by_copy[p][:, :experts]) for k in range(2)]
        for k in range(2):
            aims_out[k, p] = aims[k]
        sums = jnp.zeros((ny, 128), F32)
        for q in range(ny):
            low, high = float(2 * q), float(2 * q + 1)
            hit = sum(((v >= low) & (v <= high)).astype(F32) for v in aims)
            sums = sums + jnp.where(lane == q, jnp.sum(hit, axis=1, keepdims=True), 0.0)
        most = jnp.maximum(most, jnp.sum(sums, axis=0, keepdims=True))
    largest = jnp.max(most).astype(jnp.int32)
    choice[0] = sum((largest > size).astype(jnp.int32) for size in sizes[:-1]) + 0 * largest

    for k in range(1, ny):
        send_rows(k, lax.rem(y + ny - k, ny)).wait_recv()
    for c in sent:
        c.wait_send()


def expert_kernel(
    nep, nt, width, size,
    rows, names, aims, logits, gain_in, gain_out, w_gate, w_up, w_down,
    layer_out, next_out,
    pick, flat_l, flat_r, spots, got, full, gates, ups, downs, hid, share, landed, ret_pick, ret_start,
    ret_l, ret_r, back, slots, outgoing, incoming, whole,
    g_send, g_recv, r_send, r_recv, w_local, w_send, w_recv, e_send, e_recv, f_send, f_recv,
):
    ep, tp = lax.axis_index("ep"), lax.axis_index("tp")
    nx = NX if nt > 8 else 2
    nz = nt // nx
    ny = nep // 2
    y, core = ep // 2, lax.rem(ep, 2)
    mate = 2 * y + (1 - core)
    z, x = tp // nx, lax.rem(tp, nx)
    hp = size // 2
    own_rows = GROUP // nt
    count = {"z": nz, "x": nx}

    def neighbour(axis, sign):
        if axis == "z":
            return {"ep": ep, "tp": lax.rem(z + sign + nz, nz) * nx + x}
        return {"ep": ep, "tp": z * nx + lax.rem(x + sign + nx, nx)}

    def plane_peer(k):
        return {"ep": 2 * lax.rem(y + k, ny) + core, "tp": tp}

    partner = {"ep": mate, "tp": tp}
    friends = [neighbour(axis, step) for axis, step in steps_of(nz, nx, hp)] + [partner]
    friends += [plane_peer(k) for k in range(1, ny)]
    barrier = pltpu.get_barrier_semaphore()
    for friend in friends:
        pl.semaphore_signal(barrier, inc=1, device_id=friend, device_id_type=MESH)

    def move(src, dst, send, recv, where):
        return pltpu.make_async_remote_copy(
            src_ref=src, dst_ref=dst, send_sem=send, recv_sem=recv, device_id=where, device_id_type=MESH
        )

    weights = ((w_gate, gates), (w_up, ups), (w_down, downs))
    own_weights = [
        pltpu.make_async_copy(src.at[0], dst.at[0], w_local.at[i]) for i, (src, dst) in enumerate(weights)
    ]
    for c in own_weights:
        c.start()

    low = (2 * y).astype(F32)
    aim = [aims[k, core] for k in range(2)]
    hits = [sum((v == low + c).astype(F32) for v in aim) for c in (0.0, 1.0)]
    totals = [jnp.sum(h, axis=1, keepdims=True) for h in hits]
    lower = (iota((ny, ny), 1) < iota((ny, ny), 0)).astype(F32).astype(BF16)
    offsets = [
        jnp.dot(lower, jnp.broadcast_to(t, (ny, 128)).astype(BF16), preferred_element_type=F32)
        for t in totals
    ]
    count_low = jnp.sum(totals[0], axis=0, keepdims=True)
    starts = [offsets[0], offsets[1] + count_low]
    places = [starts[c] + rank_before(hits[c]) for c in range(2)]
    for k in range(2):
        spots[k] = jnp.where(
            aim[k] == low, places[0], jnp.where(aim[k] == low + 1.0, places[1], -1.0)
        )
    for c in range(2):
        ret_start[c] = starts[c]

    left64 = left_half((CAP, 128))

    def flatten(g, carry):
        packed = rows[g].astype(F32)
        other = swap(packed)
        top = pl.ds(pl.multiple_of(g * GROUP, GROUP), CAP)
        bottom = pl.ds(pl.multiple_of(g * GROUP + CAP, CAP), CAP)
        flat_l[top, :] = jnp.where(left64, packed, 0.0).astype(BF16)
        flat_l[bottom, :] = jnp.where(left64, other, 0.0).astype(BF16)
        flat_r[top, :] = jnp.where(left64, 0.0, other).astype(BF16)
        flat_r[bottom, :] = jnp.where(left64, 0.0, packed).astype(BF16)
        return carry

    lax.fori_loop(0, ny, flatten, 0)

    def choose(q):
        line = iota((hp, 128), 0).astype(F32) + float(q * hp)

        def one(g, carry):
            hit = (spots[0, pl.ds(g, 1), :] == line) | (spots[1, pl.ds(g, 1), :] == line)
            lanes = pl.ds(pl.multiple_of(g * GROUP, GROUP), GROUP)
            pick[:, lanes] = jnp.where(hit, 1.0, 0.0).astype(BF16)
            return carry

        lax.fori_loop(0, ny, one, 0)
        return jnp.dot(pick[...], (flat_l, flat_r)[q][...], preferred_element_type=F32)

    got[0, 0] = choose(0).astype(BF16)
    got[0, 0] = (got[0, 0].astype(F32) + choose(1)).astype(BF16)

    pl.semaphore_wait(barrier, len(friends))

    mate_weights = [
        move(src.at[0], dst.at[1], w_send.at[i], w_recv.at[i], partner)
        for i, (src, dst) in enumerate(weights)
    ]

    def slot_of(axis, offset, other):
        return (offset % nz, other) if axis == "z" else (other, offset % nx)

    gathers = [gather_plan(nz, nx, hp, c) for c in range(2)]
    reduces = [reduce_plan(nz, nx, hp, c) for c in range(2)]

    def gather_copy(c, key):
        _, axis, sign, dist, other = key
        start, many = row_range(hp, sign, dist, count[axis])
        near = ring_of(axis, c, count[axis], hp)[dist]
        src, dst = slot_of(axis, sign * near, other), slot_of(axis, sign * dist, other)
        i = gathers[c][0].index(key)
        return move(
            got.at[src[0], src[1], pl.ds(start, many), :],
            got.at[dst[0], dst[1], pl.ds(start, many), :],
            g_send.at[i], g_recv.at[i], neighbour(axis, sign * (dist - near)),
        )

    def reduce_copy(c, key):
        _, axis, sign, dist, other = key
        start, many = row_range(hp, sign, dist, count[axis])
        near = ring_of(axis, c, count[axis], hp)[dist]
        src = slot_of(axis, sign * dist, other)
        i = reduces[c][0].index(key)
        return move(
            share.at[src[0], src[1], pl.ds(start, many), :],
            landed.at[pl.ds(reduces[c][2][key][0], many), :],
            r_send.at[i], r_recv.at[i], neighbour(axis, sign * (dist - near)),
        )

    def add_landed(c, key):
        _, axis, sign, dist, other = key
        start, many = row_range(hp, sign, dist, count[axis])
        at = slot_of(axis, sign * ring_of(axis, c, count[axis], hp)[dist], other)
        here, there = pl.ds(start, many), pl.ds(reduces[c][2][key][0], many)
        share[at[0], at[1], here, :] = (
            share[at[0], at[1], here, :].astype(F32) + landed[there, :].astype(F32)
        ).astype(BF16)

    core_f = core.astype(F32)

    left = left_half((hp, 128))

    def experts():
        def join(i, carry):
            p0, p1 = [
                got[lax.rem(z - t // nx + nz, nz), lax.rem(x - lax.rem(t, nx) + nx, nx)].astype(F32)
                for t in (2 * i, 2 * i + 1)
            ]
            lanes = pl.ds(pl.multiple_of(i * 128, 128), 128)
            full[0:hp, lanes] = jnp.where(left, p0, swap(p1)).astype(BF16)
            full[hp:size, lanes] = jnp.where(left, swap(p0), p1).astype(BF16)
            return carry

        lax.fori_loop(0, nt // 2, join, 0)
        tile = next(t for t in (128, 192, 64) if size % t == 0)

        def one(i, carry):
            span = pl.ds(pl.multiple_of(i * tile, tile), tile)
            value = full[span, :].astype(F32)
            scale = lax.rsqrt(jnp.sum(value * value, axis=1, keepdims=True) * (1.0 / width) + 1e-06)
            normed = (value * scale * gain_in[...]).astype(BF16)
            spot = (iota((tile, 1), 0) + i * tile).astype(F32)
            in_low = (spot < jnp.broadcast_to(count_low, (tile, 1))).astype(F32)
            mine = in_low * (1.0 - core_f) + (1.0 - in_low) * core_f
            for w, keep in ((0, mine), (1, 1.0 - mine)):
                gate = contract(normed, gates[w])
                up = contract(normed, ups[w])
                value_h = gate / (1.0 + jnp.exp(-gate)) * up
                hid[w, span, :] = jnp.where(keep > 0.5, value_h, 0.0).astype(BF16)
            return carry

        lax.fori_loop(0, size // tile, one, 0)

    def down(dz):
        lanes = pl.ds(pl.multiple_of(lax.rem(z + dz, nz) * (nx * COLS), 128), nx * COLS)
        wd = [downs[w, :, lanes] for w in range(2)]
        sides = []
        for q in range(2):
            at = slice(q * hp, (q + 1) * hp)
            sides.append(
                jnp.dot(hid[0, at, :], wd[0], preferred_element_type=F32)
                + jnp.dot(hid[1, at, :], wd[1], preferred_element_type=F32)
            )
        for i in range(nx // 2):
            top, bottom = [v[:, i * 128 : (i + 1) * 128] for v in sides]
            d0 = lax.rem(2 * i - x + nx, nx)
            d1 = lax.rem(2 * i + 1 - x + nx, nx)
            share[dz, d0] = jnp.where(left, top, swap(bottom)).astype(BF16)
            share[dz, d1] = jnp.where(left, swap(top), bottom).astype(BF16)

    for c in mate_weights:
        c.start()

    for c in range(2):

        @pl.when(core == c)
        def _(c=c):
            for kind, key in gathers[c][1]:
                if kind == "wait":
                    break
                gather_copy(c, key).start()

    half_cap = CAP // 2
    lead = (iota((half_cap, size), 1) - iota((half_cap, size), 0)).astype(F32)
    for q in range(2):
        for c in range(2):

            def mark(g, carry, q=q, c=c):
                first = ret_start[c, pl.ds(g, 1), 0:1] + float(q * half_cap)
                at = pl.ds(pl.multiple_of(g * CAP + c * half_cap, half_cap), half_cap)
                ret_pick[q, at, :] = jnp.where(lead == first, 1.0, 0.0).astype(BF16)
                return carry

            lax.fori_loop(0, ny, mark, 0)

    for c in range(2):

        @pl.when(core == c)
        def _(c=c):
            begun = False
            for kind, key in gathers[c][1]:
                begun = begun or kind == "wait"
                if kind == "wait":
                    gather_copy(c, key).wait_recv()
                elif begun:
                    gather_copy(c, key).start()

    for c in own_weights:
        c.wait()
    for c in mate_weights:
        c.wait_recv()
    experts()

    runs = []
    for c in range(2):
        runs.append([])
        for kind, key in reduces[c][1]:
            if kind == "task":
                runs[c].append((key[1], []))
            else:
                runs[c][-1][1].append((kind, key))
    for stage in range(nz):
        assert runs[0][stage][0] == runs[1][stage][0]
        down(runs[0][stage][0])
        for c in range(2):

            @pl.when(core == c)
            def _(c=c, stage=stage):
                for kind, key in runs[c][stage][1]:
                    if kind == "start":
                        reduce_copy(c, key).start()
                    else:
                        reduce_copy(c, key).wait_recv()
                        add_landed(c, key)

    v = share[0, 0].astype(F32)
    w = swap(v)
    ret_l[0:hp, :] = jnp.where(left, v, 0.0).astype(BF16)
    ret_l[hp : 2 * hp, :] = jnp.where(left, w, 0.0).astype(BF16)
    ret_r[0:hp, :] = jnp.where(left, 0.0, w).astype(BF16)
    ret_r[hp : 2 * hp, :] = jnp.where(left, 0.0, v).astype(BF16)
    blocks = jnp.dot(ret_pick[0], ret_l[...], preferred_element_type=F32)
    blocks = blocks + jnp.dot(ret_pick[1], ret_r[...], preferred_element_type=F32)
    back[...] = blocks.astype(BF16).reshape(ny, CAP, 128)

    def return_copy(k, to, came):
        return move(back.at[to], slots.at[came], e_send.at[k], e_recv.at[k], plane_peer(k))

    returns = [
        return_copy(k, lax.rem(y + k, ny), y)
        for k in sorted(range(1, ny), key=lambda k: -min(k, ny - k))
    ]
    for c in returns:
        c.start()
    slots[y] = back[y]
    for c in mate_weights:
        c.wait_send()
    for c in range(2):

        @pl.when(core == c)
        def _(c=c):
            for key in gathers[c][0]:
                gather_copy(c, key).wait_send()
            for key in reduces[c][0]:
                reduce_copy(c, key).wait_send()


    own_ids = names[core, y].astype(F32)
    experts_all = logits.shape[0]
    which = iota((experts_all, GROUP), 0).astype(F32)
    named = [jnp.broadcast_to(own_ids[k : k + 1, :], (experts_all, GROUP)) == which for k in range(2)]
    own_before = rank_before(named[0].astype(F32) + named[1].astype(F32))
    score = logits[...]
    chosen = [jnp.sum(jnp.where(m, score, 0.0), axis=0, keepdims=True) for m in named]
    ranks = [jnp.sum(jnp.where(m, own_before, 0.0), axis=0, keepdims=True) for m in named]
    own_aims = [aims[k, core, pl.ds(y, 1), :] for k in range(2)]
    places_own = [
        jnp.where(r >= float(half_cap), float((nep - 1) * half_cap), 0.0) + t * float(half_cap) + r
        for r, t in zip(ranks, own_aims)
    ]
    shares = [
        1.0 / (1.0 + jnp.exp(chosen[1] - chosen[0])),
        1.0 / (1.0 + jnp.exp(chosen[0] - chosen[1])),
    ]
    table = jnp.concatenate(places_own + shares + [jnp.zeros((4, GROUP), F32)], axis=0).T
    lane = iota((GROUP, nep * CAP), 1).astype(F32)
    takes = [jnp.where(lane == table[:, k : k + 1], 1.0, 0.0).astype(BF16) for k in range(2)]

    for k in range(1, ny):
        return_copy(k, y, lax.rem(y + ny - k, ny)).wait_recv()
    arrived = slots[...].reshape(ny * CAP, 128).astype(F32)
    left_slots = left_half(arrived.shape)
    stacked = jnp.concatenate(
        [jnp.where(left_slots, arrived, 0.0), jnp.where(left_slots, swap(arrived), 0.0)], axis=0
    ).astype(BF16)
    mixture = table[:, 2:3] * jnp.dot(takes[0], stacked, preferred_element_type=F32)
    mixture = mixture + table[:, 3:4] * jnp.dot(takes[1], stacked, preferred_element_type=F32)
    own_packed = rows[y].astype(F32)
    layer = jnp.concatenate([own_packed, swap(own_packed)], axis=0) + mixture
    for t in range(nt):
        outgoing[t] = layer[t * own_rows : (t + 1) * own_rows, :].astype(BF16)

    def owner_copy(k, to, came):
        where = {"ep": ep, "tp": lax.rem(tp + k, nt)}
        return move(outgoing.at[to], incoming.at[came], f_send.at[k], f_recv.at[k], where)

    def hops(k):
        return min(k // nx, nz - k // nx) + min(k % nx, nx - k % nx)

    owners = [
        owner_copy(k, lax.rem(tp + k, nt), tp) for k in sorted(range(1, nt), key=lambda k: -hops(k))
    ]
    for c in owners:
        c.start()
    incoming[tp] = outgoing[tp]
    for c in returns + owners:
        c.wait_send()
    for k in range(1, nt):
        owner_copy(k, tp, lax.rem(tp + nt - k, nt)).wait_recv()
    left_own = left_half((own_rows, 128))
    for i in range(nt // 2):
        v0, v1 = incoming[2 * i].astype(F32), incoming[2 * i + 1].astype(F32)
        whole[:, i * 128 : (i + 1) * 128] = jnp.where(left_own, v0, swap(v1))
    value = whole[...]
    layer_out[...] = value.astype(BF16)
    scale = lax.rsqrt(jnp.sum(value * value, axis=1, keepdims=True) * (1.0 / width) + 1e-06)
    next_out[...] = (value * scale * gain_out[...]).astype(BF16)


def collect(attn_out, w_out, residual_in, ids, copies, nep, nt, sizes):
    vmem = pl.BlockSpec(memory_space=pltpu.VMEM)
    ny = nep // 2
    dma = pltpu.SemaphoreType.DMA
    return pl.pallas_call(
        functools.partial(collect_kernel, nep, nt, sizes),
        out_shape=(
            jax.ShapeDtypeStruct((ny, CAP, 128), BF16),
            jax.ShapeDtypeStruct((2, ny, 16, 128), BF16),
            jax.ShapeDtypeStruct((2, 2, ny, 128), F32),
            jax.ShapeDtypeStruct((1,), jnp.int32),
        ),
        in_specs=[vmem, vmem, pl.BlockSpec(memory_space=pl.ANY), vmem, vmem],
        out_specs=(vmem, vmem, vmem, pl.BlockSpec(memory_space=pltpu.SMEM)),
        scratch_shapes=[
            pltpu.VMEM((GROUP, 128), BF16),
            pltpu.VMEM((128, 8), F32),
            dma((1,)),
            dma((nep + ny,)),
            dma((nep + ny,)),
        ],
        compiler_params=pltpu.CompilerParams(collective_id=0, has_side_effects=True),
        name="collect",
    )(attn_out, w_out, residual_in, ids, copies)


def experts_call(size, which, nep, nt, rows, names, aims, logits, gain_in, gain_out, w_gate, w_up, w_down):
    vmem = pl.BlockSpec(memory_space=pltpu.VMEM)
    hbm = pl.BlockSpec(memory_space=pl.ANY)
    inner, width = w_gate.shape[1], w_gate.shape[2]
    nx = NX if nt > 8 else 2
    nz = nt // nx
    ny = nep // 2
    hp = size // 2
    own_rows = GROUP // nt
    many = len(gather_plan(nz, nx, hp, 0)[0]), len(gather_plan(nz, nx, hp, 1)[0])
    land = max(reduce_plan(nz, nx, hp, c)[3] for c in range(2))
    dma = pltpu.SemaphoreType.DMA
    out = jax.ShapeDtypeStruct((own_rows, width), BF16)
    return pl.pallas_call(
        functools.partial(expert_kernel, nep, nt, width, size),
        out_shape=(out, out),
        in_specs=[vmem] * 6 + [hbm] * 3,
        out_specs=(vmem, vmem),
        scratch_shapes=[
            pltpu.VMEM((hp, ny * GROUP), BF16),
            pltpu.VMEM((ny * GROUP, 128), BF16),
            pltpu.VMEM((ny * GROUP, 128), BF16),
            pltpu.VMEM((2, ny, 128), F32),
            pltpu.VMEM((nz, nx, hp, 128), BF16),
            pltpu.VMEM((size, width), BF16),
            pltpu.VMEM((2, inner, width), BF16),
            pltpu.VMEM((2, inner, width), BF16),
            pltpu.VMEM((2, inner, width), BF16),
            pltpu.VMEM((2, size, inner), BF16),
            pltpu.VMEM((nz, nx, hp, 128), BF16),
            pltpu.VMEM((land, 128), BF16),
            pltpu.VMEM((2, ny * CAP, size), BF16),
            pltpu.VMEM((2, ny, 128), F32),
            pltpu.VMEM((size, 128), BF16),
            pltpu.VMEM((size, 128), BF16),
            pltpu.VMEM((ny, CAP, 128), BF16),
            pltpu.VMEM((ny, CAP, 128), BF16),
            pltpu.VMEM((nt, own_rows, 128), BF16),
            pltpu.VMEM((nt, own_rows, 128), BF16),
            pltpu.VMEM((own_rows, width), F32),
            dma((max(many),)), dma((max(many),)),
            dma((max(many),)), dma((max(many),)),
            dma((3,)), dma((3,)), dma((3,)),
            dma((ny,)), dma((ny,)),
            dma((nt,)), dma((nt,)),
        ],
        compiler_params=pltpu.CompilerParams(
            collective_id=which, has_side_effects=True, vmem_limit_bytes=60 * 2**20
        ),
        name="experts_%d" % size,
    )(rows, names, aims, logits, gain_in, gain_out, w_gate, w_up, w_down)


def per_device(sizes, attn_out, residual_in, w_out, gain_in, router_logits, expert_ids, copy_of, w_gate, w_up, w_down, gain_out):
    nt, nep = lax.axis_size("tp"), lax.axis_size("ep")
    rows, names, aims, choice = collect(
        attn_out, w_out.T, residual_in, expert_ids.T, copy_of.T, nep, nt, sizes
    )
    operands = (
        rows, names, aims, router_logits.T, gain_in[None, :], gain_out[None, :],
        jnp.swapaxes(w_gate, 1, 2), jnp.swapaxes(w_up, 1, 2), w_down,
    )
    branches = [
        functools.partial(experts_call, size, i + 1, nep, nt) for i, size in enumerate(sizes)
    ]
    if len(branches) == 1:
        return branches[0](*operands)
    return lax.switch(choice[0], branches, *operands)


def solution(mesh, sizes=(512, 640, 768, 1024)):
    return jax.shard_map(
        functools.partial(per_device, sizes),
        mesh=mesh,
        in_specs=(
            P("ep", None),
            P("ep", None),
            P(None, "tp"),
            P(),
            P("ep", None),
            P("ep", None),
            P(),
            P("ep", None, "tp"),
            P("ep", None, "tp"),
            P("ep", "tp", None),
            P(),
        ),
        out_specs=(P(("ep", "tp"), None), P(("ep", "tp"), None)),
        check_vma=False,
    )
```

```python
import functools
import heapq

import jax
import jax.numpy as jnp
from jax import lax
from jax.experimental import pallas as pl
from jax.experimental.pallas import tpu as pltpu
from jax.sharding import PartitionSpec as P

MESH = pl.DeviceIdType.MESH
F32 = jnp.float32
BF16 = jnp.bfloat16
NX = 4
COLS = 64
GROUP = 128
CAP = 64
SIGNS = (1, -1)


def row_range(rows, sign, dist, count):
    if 2 * dist == count:
        half = rows // 2
        return (0, half) if sign > 0 else (half, half)
    return (0, rows)


AXES = (("z", "x"), ("x", "z"))
NEXT = {1: 0, 2: 1, 3: 2, 4: 3}
PAIR = {1: 0, 2: 0, 3: 2, 4: 2}


def ring_of(axis, core, n, rows):
    if axis == "z":
        ring = PAIR if core == 0 and rows <= 256 else NEXT
    else:
        ring = PAIR if core == 0 or rows <= 320 else NEXT
    return {d: p for d, p in ring.items() if 2 * d <= n}


def steps_of(nz, nx, rows):
    found = set()
    for core in range(2):
        for axis, n in (("z", nz), ("x", nx)):
            for dist, near in ring_of(axis, core, n, rows).items():
                for sign in SIGNS:
                    found.add((axis, sign * (dist - near) % n))
    return sorted(found)


def gather_sends(nz, nx, rows, core):
    count, sends = {"z": nz, "x": nx}, {}
    first, second = AXES[core]
    for axis in (first, second):
        n = count[axis]
        ring = ring_of(axis, core, n, rows)
        for other in range(1 if axis == first else count[first]):
            for dist, near in ring.items():
                for sign in SIGNS:
                    need = set()
                    if near:
                        need.add(("g", axis, sign, near, other))
                    elif axis == second and other:
                        m = count[first]
                        if 2 * other <= m:
                            need.add(("g", first, 1, other, 0))
                        if 2 * other >= m:
                            need.add(("g", first, -1, m - other, 0))
                    size = row_range(rows, sign, dist, n)[1]
                    sends[("g", axis, sign, dist, other)] = ((axis, sign), size * (dist - near), need)
    return sends


def reduce_sends(nz, nx, rows, core):
    count, sends = {"z": nz, "x": nx}, {}
    second, first = AXES[core]
    for axis in (first, second):
        n = count[axis]
        ring = ring_of(axis, core, n, rows)
        for other in range(count[second] if axis == first else 1):
            for dist in sorted(ring, reverse=True):
                for sign in SIGNS:
                    offset = (sign * dist) % n
                    need = {("c", offset if axis == "z" else other)}
                    for further, near in ring.items():
                        if near == dist:
                            need.add(("r", axis, sign, further, other))
                    if axis == second:
                        for further, near in ring_of(first, core, count[first], rows).items():
                            if near == 0:
                                for way in SIGNS:
                                    need.add(("r", first, way, further, offset))
                    size = row_range(rows, sign, dist, n)[1]
                    sends[("r", axis, sign, dist, other)] = (
                        (axis, sign), size * (dist - ring[dist]), need
                    )
    return sends


def timeline(sends, tasks):
    rate, latency = 330.0, 1.7
    done, free, ops, arrivals = set(), {}, [], []
    waiting, later, now = dict(sends), dict(tasks), 0.0

    def release():
        for key in [k for k, v in waiting.items() if v[2] <= done]:
            link, size, _ = waiting.pop(key)
            free[link] = max(now, free.get(link, 0.0)) + size / rate
            ops.append(("start", key))
            heapq.heappush(arrivals, (free[link] + latency, len(ops), key))

    release()
    while arrivals or later:
        if arrivals and arrivals[0][0] <= now:
            key = heapq.heappop(arrivals)[2]
            ops.append(("wait", key))
            now += 0.05 + (sends[key][1] * 0.0006 if key[0] == "r" else 0.0)
            done.add(key)
            release()
            continue
        able = [k for k, v in later.items() if v[1] <= done]
        if able:
            now += later.pop(able[0])[0]
            ops.append(("task", able[0]))
            done.add(able[0])
            release()
            continue
        now = max(now, arrivals[0][0])
    assert not waiting
    return ops


def gather_plan(nz, nx, rows, core):
    sends = gather_sends(nz, nx, rows, core)
    return list(sends), timeline(sends, {})


def reduce_plan(nz, nx, rows, core):
    sends = reduce_sends(nz, nx, rows, core)
    tasks, before = {}, set()
    for dz in sorted(range(nz), key=lambda d: (-min(d, nz - d), d)):
        tasks[("c", dz)] = (rows * 0.0009, before)
        before = {("c", dz)}
    landing, total = {}, 0
    for key, value in sends.items():
        many = row_range(rows, key[2], key[3], nz if key[1] == "z" else nx)[1]
        landing[key] = (total, many)
        total += many
    return list(sends), timeline(sends, tasks), landing, total


def iota(shape, dim):
    return lax.broadcasted_iota(jnp.int32, shape, dim)


def left_half(shape):
    return iota(shape, len(shape) - 1) < COLS


def swap(value):
    return pltpu.roll(value, COLS, value.ndim - 1)


def rank_before(hits):
    tri = (iota((GROUP, GROUP), 0) < iota((GROUP, GROUP), 1)).astype(F32).astype(BF16)
    return jnp.dot(hits.astype(BF16), tri, preferred_element_type=F32)


def targets_of(ids, copies):
    experts = copies.shape[1]
    total = jnp.zeros(ids.shape, F32)
    for e in range(experts):
        total = total + jnp.where(ids == float(e), copies[:, e : e + 1], 0.0)
    return total


def contract(lhs, rhs):
    return lax.dot_general(lhs, rhs, (((1,), (1,)), ((), ())), preferred_element_type=F32)


def collect_kernel(
    nep, nt, sizes,
    attn, w_out, residual, ids, copies,
    rows_out, names_out, aims_out, choice,
    columns, by_group, local_sem, send_sem, recv_sem,
):
    ep, tp = lax.axis_index("ep"), lax.axis_index("tp")
    ny = nep // 2
    y, core = ep // 2, lax.rem(ep, 2)

    barrier = pltpu.get_barrier_semaphore()
    for k in range(1, nep):
        pl.semaphore_signal(
            barrier, inc=1, device_id={"ep": lax.rem(ep + k, nep), "tp": tp}, device_id_type=MESH
        )
    fetch = pltpu.make_async_copy(
        residual.at[:, pl.ds(pl.multiple_of((tp // 2) * 128, 128), 128)], columns, local_sem.at[0]
    )
    fetch.start()
    names = ids[...].astype(F32)
    names_out[core, y] = jnp.concatenate([names, jnp.zeros((14, GROUP), F32)], axis=0).astype(BF16)
    experts = copies.shape[0]
    padded = jnp.concatenate([copies[...].astype(F32), jnp.zeros((experts, 128 - nep), F32)], axis=1)
    if experts < 8:
        padded = jnp.concatenate([padded, jnp.zeros((8 - experts, 128), F32)], axis=0)
    by_group[...] = padded.T
    product = contract(attn[...], w_out[...]).astype(BF16).astype(F32)
    fetch.wait()
    pair = columns[...].astype(F32)
    left = left_half((CAP, 128))
    pair = jnp.where(lax.rem(tp, 2) == 1, swap(pair), pair)
    carried = pair + jnp.concatenate([product, product], axis=1)
    packed = jnp.where(left, carried[:CAP], swap(carried[CAP:]))
    rows_out[y] = packed.astype(BF16)

    pl.semaphore_wait(barrier, nep - 1)

    def send_names(k, parity, plane):
        return pltpu.make_async_remote_copy(
            src_ref=names_out.at[parity, plane],
            dst_ref=names_out.at[parity, plane],
            send_sem=send_sem.at[k],
            recv_sem=recv_sem.at[k],
            device_id={"ep": lax.rem(ep + k, nep), "tp": tp},
            device_id_type=MESH,
        )

    def send_rows(k, plane):
        return pltpu.make_async_remote_copy(
            src_ref=rows_out.at[plane],
            dst_ref=rows_out.at[plane],
            send_sem=send_sem.at[nep + k],
            recv_sem=recv_sem.at[nep + k],
            device_id={"ep": 2 * lax.rem(y + k, ny) + core, "tp": tp},
            device_id_type=MESH,
        )

    sent = [send_names(k, core, y) for k in sorted(range(1, nep), key=lambda k: -min(k, nep - k))]
    sent += [send_rows(k, y) for k in sorted(range(1, ny), key=lambda k: -min(k, ny - k))]
    for c in sent:
        c.start()
    for k in range(1, nep):
        came = lax.rem(ep + nep - k, nep)
        send_names(k, lax.rem(came, 2), came // 2).wait_recv()

    table = names_out[...].astype(F32)
    by_copy = [by_group[pl.ds(p, ny, stride=2), :] for p in range(2)]
    hits = [jnp.zeros((ny, GROUP), F32) for p in range(2)]
    most = jnp.zeros((1, 128), F32)
    lane = iota((ny, 128), 1)
    for p in range(2):
        aims = [targets_of(table[p, :, k, :], by_copy[p][:, :experts]) for k in range(2)]
        for k in range(2):
            aims_out[k, p] = aims[k]
        sums = jnp.zeros((ny, 128), F32)
        for q in range(ny):
            low, high = float(2 * q), float(2 * q + 1)
            hit = sum(((v >= low) & (v <= high)).astype(F32) for v in aims)
            sums = sums + jnp.where(lane == q, jnp.sum(hit, axis=1, keepdims=True), 0.0)
        most = jnp.maximum(most, jnp.sum(sums, axis=0, keepdims=True))
    largest = jnp.max(most).astype(jnp.int32)
    choice[0] = sum((largest > size).astype(jnp.int32) for size in sizes[:-1]) + 0 * largest

    for k in range(1, ny):
        send_rows(k, lax.rem(y + ny - k, ny)).wait_recv()
    for c in sent:
        c.wait_send()


def expert_kernel(
    nep, nt, width, size,
    rows, names, aims, logits, gain_in, gain_out, w_gate, w_up, w_down,
    layer_out, next_out,
    pick, flat_l, flat_r, spots, got, full, gates, ups, downs, hid, share, landed, ret_pick, ret_start,
    ret_l, ret_r, back, slots, outgoing, incoming, whole,
    g_send, g_recv, r_send, r_recv, w_local, w_send, w_recv, e_send, e_recv, f_send, f_recv,
):
    ep, tp = lax.axis_index("ep"), lax.axis_index("tp")
    nx = NX if nt > 8 else 2
    nz = nt // nx
    ny = nep // 2
    y, core = ep // 2, lax.rem(ep, 2)
    mate = 2 * y + (1 - core)
    z, x = tp // nx, lax.rem(tp, nx)
    hp = size // 2
    own_rows = GROUP // nt
    count = {"z": nz, "x": nx}

    def neighbour(axis, sign):
        if axis == "z":
            return {"ep": ep, "tp": lax.rem(z + sign + nz, nz) * nx + x}
        return {"ep": ep, "tp": z * nx + lax.rem(x + sign + nx, nx)}

    def plane_peer(k):
        return {"ep": 2 * lax.rem(y + k, ny) + core, "tp": tp}

    partner = {"ep": mate, "tp": tp}
    friends = [neighbour(axis, step) for axis, step in steps_of(nz, nx, hp)] + [partner]
    friends += [plane_peer(k) for k in range(1, ny)]
    barrier = pltpu.get_barrier_semaphore()
    for friend in friends:
        pl.semaphore_signal(barrier, inc=1, device_id=friend, device_id_type=MESH)

    def move(src, dst, send, recv, where):
        return pltpu.make_async_remote_copy(
            src_ref=src, dst_ref=dst, send_sem=send, recv_sem=recv, device_id=where, device_id_type=MESH
        )

    weights = ((w_gate, gates), (w_up, ups), (w_down, downs))
    own_weights = [
        pltpu.make_async_copy(src.at[0], dst.at[0], w_local.at[i]) for i, (src, dst) in enumerate(weights)
    ]
    for c in own_weights:
        c.start()

    low = (2 * y).astype(F32)
    aim = [aims[k, core] for k in range(2)]
    hits = [sum((v == low + c).astype(F32) for v in aim) for c in (0.0, 1.0)]
    totals = [jnp.sum(h, axis=1, keepdims=True) for h in hits]
    lower = (iota((ny, ny), 1) < iota((ny, ny), 0)).astype(F32).astype(BF16)
    offsets = [
        jnp.dot(lower, jnp.broadcast_to(t, (ny, 128)).astype(BF16), preferred_element_type=F32)
        for t in totals
    ]
    count_low = jnp.sum(totals[0], axis=0, keepdims=True)
    starts = [offsets[0], offsets[1] + count_low]
    places = [starts[c] + rank_before(hits[c]) for c in range(2)]
    for k in range(2):
        spots[k] = jnp.where(
            aim[k] == low, places[0], jnp.where(aim[k] == low + 1.0, places[1], -1.0)
        )
    for c in range(2):
        ret_start[c] = starts[c]

    left64 = left_half((CAP, 128))

    def flatten(g, carry):
        packed = rows[g].astype(F32)
        other = swap(packed)
        top = pl.ds(pl.multiple_of(g * GROUP, GROUP), CAP)
        bottom = pl.ds(pl.multiple_of(g * GROUP + CAP, CAP), CAP)
        flat_l[top, :] = jnp.where(left64, packed, 0.0).astype(BF16)
        flat_l[bottom, :] = jnp.where(left64, other, 0.0).astype(BF16)
        flat_r[top, :] = jnp.where(left64, 0.0, other).astype(BF16)
        flat_r[bottom, :] = jnp.where(left64, 0.0, packed).astype(BF16)
        return carry

    lax.fori_loop(0, ny, flatten, 0)

    def choose(q):
        line = iota((hp, 128), 0).astype(F32) + float(q * hp)

        def one(g, carry):
            hit = (spots[0, pl.ds(g, 1), :] == line) | (spots[1, pl.ds(g, 1), :] == line)
            lanes = pl.ds(pl.multiple_of(g * GROUP, GROUP), GROUP)
            pick[:, lanes] = jnp.where(hit, 1.0, 0.0).astype(BF16)
            return carry

        lax.fori_loop(0, ny, one, 0)
        return jnp.dot(pick[...], (flat_l, flat_r)[q][...], preferred_element_type=F32)

    got[0, 0] = choose(0).astype(BF16)
    got[0, 0] = (got[0, 0].astype(F32) + choose(1)).astype(BF16)

    pl.semaphore_wait(barrier, len(friends))

    mate_weights = [
        move(src.at[0], dst.at[1], w_send.at[i], w_recv.at[i], partner)
        for i, (src, dst) in enumerate(weights)
    ]

    def slot_of(axis, offset, other):
        return (offset % nz, other) if axis == "z" else (other, offset % nx)

    gathers = [gather_plan(nz, nx, hp, c) for c in range(2)]
    reduces = [reduce_plan(nz, nx, hp, c) for c in range(2)]

    def gather_copy(c, key):
        _, axis, sign, dist, other = key
        start, many = row_range(hp, sign, dist, count[axis])
        near = ring_of(axis, c, count[axis], hp)[dist]
        src, dst = slot_of(axis, sign * near, other), slot_of(axis, sign * dist, other)
        i = gathers[c][0].index(key)
        return move(
            got.at[src[0], src[1], pl.ds(start, many), :],
            got.at[dst[0], dst[1], pl.ds(start, many), :],
            g_send.at[i], g_recv.at[i], neighbour(axis, sign * (dist - near)),
        )

    def reduce_copy(c, key):
        _, axis, sign, dist, other = key
        start, many = row_range(hp, sign, dist, count[axis])
        near = ring_of(axis, c, count[axis], hp)[dist]
        src = slot_of(axis, sign * dist, other)
        i = reduces[c][0].index(key)
        return move(
            share.at[src[0], src[1], pl.ds(start, many), :],
            landed.at[pl.ds(reduces[c][2][key][0], many), :],
            r_send.at[i], r_recv.at[i], neighbour(axis, sign * (dist - near)),
        )

    def add_landed(c, key):
        _, axis, sign, dist, other = key
        start, many = row_range(hp, sign, dist, count[axis])
        at = slot_of(axis, sign * ring_of(axis, c, count[axis], hp)[dist], other)
        here, there = pl.ds(start, many), pl.ds(reduces[c][2][key][0], many)
        share[at[0], at[1], here, :] = (
            share[at[0], at[1], here, :].astype(F32) + landed[there, :].astype(F32)
        ).astype(BF16)

    core_f = core.astype(F32)

    left = left_half((hp, 128))

    def experts():
        def join(i, carry):
            p0, p1 = [
                got[lax.rem(z - t // nx + nz, nz), lax.rem(x - lax.rem(t, nx) + nx, nx)].astype(F32)
                for t in (2 * i, 2 * i + 1)
            ]
            lanes = pl.ds(pl.multiple_of(i * 128, 128), 128)
            full[0:hp, lanes] = jnp.where(left, p0, swap(p1)).astype(BF16)
            full[hp:size, lanes] = jnp.where(left, swap(p0), p1).astype(BF16)
            return carry

        lax.fori_loop(0, nt // 2, join, 0)
        tile = next(t for t in (128, 192, 64) if size % t == 0)

        def one(i, carry):
            span = pl.ds(pl.multiple_of(i * tile, tile), tile)
            value = full[span, :].astype(F32)
            scale = lax.rsqrt(jnp.sum(value * value, axis=1, keepdims=True) * (1.0 / width) + 1e-06)
            normed = (value * scale * gain_in[...]).astype(BF16)
            spot = (iota((tile, 1), 0) + i * tile).astype(F32)
            in_low = (spot < jnp.broadcast_to(count_low, (tile, 1))).astype(F32)
            mine = in_low * (1.0 - core_f) + (1.0 - in_low) * core_f
            for w, keep in ((0, mine), (1, 1.0 - mine)):
                gate = contract(normed, gates[w])
                up = contract(normed, ups[w])
                value_h = gate / (1.0 + jnp.exp(-gate)) * up
                hid[w, span, :] = jnp.where(keep > 0.5, value_h, 0.0).astype(BF16)
            return carry

        lax.fori_loop(0, size // tile, one, 0)

    def down(dz):
        lanes = pl.ds(pl.multiple_of(lax.rem(z + dz, nz) * (nx * COLS), 128), nx * COLS)
        wd = [downs[w, :, lanes] for w in range(2)]
        sides = []
        for q in range(2):
            at = slice(q * hp, (q + 1) * hp)
            sides.append(
                jnp.dot(hid[0, at, :], wd[0], preferred_element_type=F32)
                + jnp.dot(hid[1, at, :], wd[1], preferred_element_type=F32)
            )
        for i in range(nx // 2):
            top, bottom = [v[:, i * 128 : (i + 1) * 128] for v in sides]
            d0 = lax.rem(2 * i - x + nx, nx)
            d1 = lax.rem(2 * i + 1 - x + nx, nx)
            share[dz, d0] = jnp.where(left, top, swap(bottom)).astype(BF16)
            share[dz, d1] = jnp.where(left, swap(top), bottom).astype(BF16)

    for c in mate_weights:
        c.start()

    for c in range(2):

        @pl.when(core == c)
        def _(c=c):
            for kind, key in gathers[c][1]:
                if kind == "wait":
                    break
                gather_copy(c, key).start()

    half_cap = CAP // 2
    lead = (iota((half_cap, size), 1) - iota((half_cap, size), 0)).astype(F32)
    for q in range(2):
        for c in range(2):

            def mark(g, carry, q=q, c=c):
                first = ret_start[c, pl.ds(g, 1), 0:1] + float(q * half_cap)
                at = pl.ds(pl.multiple_of(g * CAP + c * half_cap, half_cap), half_cap)
                ret_pick[q, at, :] = jnp.where(lead == first, 1.0, 0.0).astype(BF16)
                return carry

            lax.fori_loop(0, ny, mark, 0)

    for c in range(2):

        @pl.when(core == c)
        def _(c=c):
            begun = False
            for kind, key in gathers[c][1]:
                begun = begun or kind == "wait"
                if kind == "wait":
                    gather_copy(c, key).wait_recv()
                elif begun:
                    gather_copy(c, key).start()

    for c in own_weights:
        c.wait()
    for c in mate_weights:
        c.wait_recv()
    experts()

    runs = []
    for c in range(2):
        runs.append([])
        for kind, key in reduces[c][1]:
            if kind == "task":
                runs[c].append((key[1], []))
            else:
                runs[c][-1][1].append((kind, key))
    for stage in range(nz):
        assert runs[0][stage][0] == runs[1][stage][0]
        down(runs[0][stage][0])
        for c in range(2):

            @pl.when(core == c)
            def _(c=c, stage=stage):
                for kind, key in runs[c][stage][1]:
                    if kind == "start":
                        reduce_copy(c, key).start()
                    else:
                        reduce_copy(c, key).wait_recv()
                        add_landed(c, key)

    v = share[0, 0].astype(F32)
    w = swap(v)
    ret_l[0:hp, :] = jnp.where(left, v, 0.0).astype(BF16)
    ret_l[hp : 2 * hp, :] = jnp.where(left, w, 0.0).astype(BF16)
    ret_r[0:hp, :] = jnp.where(left, 0.0, w).astype(BF16)
    ret_r[hp : 2 * hp, :] = jnp.where(left, 0.0, v).astype(BF16)
    blocks = jnp.dot(ret_pick[0], ret_l[...], preferred_element_type=F32)
    blocks = blocks + jnp.dot(ret_pick[1], ret_r[...], preferred_element_type=F32)
    back[...] = blocks.astype(BF16).reshape(ny, CAP, 128)

    def return_copy(k, to, came):
        return move(back.at[to], slots.at[came], e_send.at[k], e_recv.at[k], plane_peer(k))

    returns = [
        return_copy(k, lax.rem(y + k, ny), y)
        for k in sorted(range(1, ny), key=lambda k: -min(k, ny - k))
    ]
    for c in returns:
        c.start()
    slots[y] = back[y]
    for c in mate_weights:
        c.wait_send()
    for c in range(2):

        @pl.when(core == c)
        def _(c=c):
            for key in gathers[c][0]:
                gather_copy(c, key).wait_send()
            for key in reduces[c][0]:
                reduce_copy(c, key).wait_send()


    own_ids = names[core, y].astype(F32)
    experts_all = logits.shape[0]
    which = iota((experts_all, GROUP), 0).astype(F32)
    named = [jnp.broadcast_to(own_ids[k : k + 1, :], (experts_all, GROUP)) == which for k in range(2)]
    own_before = rank_before(named[0].astype(F32) + named[1].astype(F32))
    score = logits[...]
    chosen = [jnp.sum(jnp.where(m, score, 0.0), axis=0, keepdims=True) for m in named]
    ranks = [jnp.sum(jnp.where(m, own_before, 0.0), axis=0, keepdims=True) for m in named]
    own_aims = [aims[k, core, pl.ds(y, 1), :] for k in range(2)]
    places_own = [
        jnp.where(r >= float(half_cap), float((nep - 1) * half_cap), 0.0) + t * float(half_cap) + r
        for r, t in zip(ranks, own_aims)
    ]
    shares = [
        1.0 / (1.0 + jnp.exp(chosen[1] - chosen[0])),
        1.0 / (1.0 + jnp.exp(chosen[0] - chosen[1])),
    ]
    table = jnp.concatenate(places_own + shares + [jnp.zeros((4, GROUP), F32)], axis=0).T
    lane = iota((GROUP, nep * CAP), 1).astype(F32)
    takes = [jnp.where(lane == table[:, k : k + 1], 1.0, 0.0).astype(BF16) for k in range(2)]

    for k in range(1, ny):
        return_copy(k, y, lax.rem(y + ny - k, ny)).wait_recv()
    arrived = slots[...].reshape(ny * CAP, 128).astype(F32)
    left_slots = left_half(arrived.shape)
    stacked = jnp.concatenate(
        [jnp.where(left_slots, arrived, 0.0), jnp.where(left_slots, swap(arrived), 0.0)], axis=0
    ).astype(BF16)
    mixture = table[:, 2:3] * jnp.dot(takes[0], stacked, preferred_element_type=F32)
    mixture = mixture + table[:, 3:4] * jnp.dot(takes[1], stacked, preferred_element_type=F32)
    own_packed = rows[y].astype(F32)
    layer = jnp.concatenate([own_packed, swap(own_packed)], axis=0) + mixture
    for t in range(nt):
        outgoing[t] = layer[t * own_rows : (t + 1) * own_rows, :].astype(BF16)

    def owner_copy(k, to, came):
        where = {"ep": ep, "tp": lax.rem(tp + k, nt)}
        return move(outgoing.at[to], incoming.at[came], f_send.at[k], f_recv.at[k], where)

    def hops(k):
        return min(k // nx, nz - k // nx) + min(k % nx, nx - k % nx)

    owners = [
        owner_copy(k, lax.rem(tp + k, nt), tp) for k in sorted(range(1, nt), key=lambda k: -hops(k))
    ]
    for c in owners:
        c.start()
    incoming[tp] = outgoing[tp]
    for c in returns + owners:
        c.wait_send()
    for k in range(1, nt):
        owner_copy(k, tp, lax.rem(tp + nt - k, nt)).wait_recv()
    left_own = left_half((own_rows, 128))
    for i in range(nt // 2):
        v0, v1 = incoming[2 * i].astype(F32), incoming[2 * i + 1].astype(F32)
        whole[:, i * 128 : (i + 1) * 128] = jnp.where(left_own, v0, swap(v1))
    value = whole[...]
    layer_out[...] = value.astype(BF16)
    scale = lax.rsqrt(jnp.sum(value * value, axis=1, keepdims=True) * (1.0 / width) + 1e-06)
    next_out[...] = (value * scale * gain_out[...]).astype(BF16)


def collect(attn_out, w_out, residual_in, ids, copies, nep, nt, sizes):
    vmem = pl.BlockSpec(memory_space=pltpu.VMEM)
    ny = nep // 2
    dma = pltpu.SemaphoreType.DMA
    return pl.pallas_call(
        functools.partial(collect_kernel, nep, nt, sizes),
        out_shape=(
            jax.ShapeDtypeStruct((ny, CAP, 128), BF16),
            jax.ShapeDtypeStruct((2, ny, 16, 128), BF16),
            jax.ShapeDtypeStruct((2, 2, ny, 128), F32),
            jax.ShapeDtypeStruct((1,), jnp.int32),
        ),
        in_specs=[vmem, vmem, pl.BlockSpec(memory_space=pl.ANY), vmem, vmem],
        out_specs=(vmem, vmem, vmem, pl.BlockSpec(memory_space=pltpu.SMEM)),
        scratch_shapes=[
            pltpu.VMEM((GROUP, 128), BF16),
            pltpu.VMEM((128, 8), F32),
            dma((1,)),
            dma((nep + ny,)),
            dma((nep + ny,)),
        ],
        compiler_params=pltpu.CompilerParams(collective_id=0, has_side_effects=True),
        name="collect",
    )(attn_out, w_out, residual_in, ids, copies)


def experts_call(size, which, nep, nt, rows, names, aims, logits, gain_in, gain_out, w_gate, w_up, w_down):
    vmem = pl.BlockSpec(memory_space=pltpu.VMEM)
    hbm = pl.BlockSpec(memory_space=pl.ANY)
    inner, width = w_gate.shape[1], w_gate.shape[2]
    nx = NX if nt > 8 else 2
    nz = nt // nx
    ny = nep // 2
    hp = size // 2
    own_rows = GROUP // nt
    many = len(gather_plan(nz, nx, hp, 0)[0]), len(gather_plan(nz, nx, hp, 1)[0])
    land = max(reduce_plan(nz, nx, hp, c)[3] for c in range(2))
    dma = pltpu.SemaphoreType.DMA
    out = jax.ShapeDtypeStruct((own_rows, width), BF16)
    return pl.pallas_call(
        functools.partial(expert_kernel, nep, nt, width, size),
        out_shape=(out, out),
        in_specs=[vmem] * 6 + [hbm] * 3,
        out_specs=(vmem, vmem),
        scratch_shapes=[
            pltpu.VMEM((hp, ny * GROUP), BF16),
            pltpu.VMEM((ny * GROUP, 128), BF16),
            pltpu.VMEM((ny * GROUP, 128), BF16),
            pltpu.VMEM((2, ny, 128), F32),
            pltpu.VMEM((nz, nx, hp, 128), BF16),
            pltpu.VMEM((size, width), BF16),
            pltpu.VMEM((2, inner, width), BF16),
            pltpu.VMEM((2, inner, width), BF16),
            pltpu.VMEM((2, inner, width), BF16),
            pltpu.VMEM((2, size, inner), BF16),
            pltpu.VMEM((nz, nx, hp, 128), BF16),
            pltpu.VMEM((land, 128), BF16),
            pltpu.VMEM((2, ny * CAP, size), BF16),
            pltpu.VMEM((2, ny, 128), F32),
            pltpu.VMEM((size, 128), BF16),
            pltpu.VMEM((size, 128), BF16),
            pltpu.VMEM((ny, CAP, 128), BF16),
            pltpu.VMEM((ny, CAP, 128), BF16),
            pltpu.VMEM((nt, own_rows, 128), BF16),
            pltpu.VMEM((nt, own_rows, 128), BF16),
            pltpu.VMEM((own_rows, width), F32),
            dma((max(many),)), dma((max(many),)),
            dma((max(many),)), dma((max(many),)),
            dma((3,)), dma((3,)), dma((3,)),
            dma((ny,)), dma((ny,)),
            dma((nt,)), dma((nt,)),
        ],
        compiler_params=pltpu.CompilerParams(
            collective_id=which, has_side_effects=True, vmem_limit_bytes=60 * 2**20
        ),
        name="experts_%d" % size,
    )(rows, names, aims, logits, gain_in, gain_out, w_gate, w_up, w_down)


def per_device(sizes, attn_out, residual_in, w_out, gain_in, router_logits, expert_ids, copy_of, w_gate, w_up, w_down, gain_out):
    nt, nep = lax.axis_size("tp"), lax.axis_size("ep")
    rows, names, aims, choice = collect(
        attn_out, w_out.T, residual_in, expert_ids.T, copy_of.T, nep, nt, sizes
    )
    operands = (
        rows, names, aims, router_logits.T, gain_in[None, :], gain_out[None, :],
        jnp.swapaxes(w_gate, 1, 2), jnp.swapaxes(w_up, 1, 2), w_down,
    )
    branches = [
        functools.partial(experts_call, size, i + 1, nep, nt) for i, size in enumerate(sizes)
    ]
    if len(branches) == 1:
        return branches[0](*operands)
    return lax.switch(choice[0], branches, *operands)


def solution(mesh, sizes=(512, 640, 768, 1024)):
    return jax.shard_map(
        functools.partial(per_device, sizes),
        mesh=mesh,
        in_specs=(
            P("ep", None),
            P("ep", None),
            P(None, "tp"),
            P(),
            P("ep", None),
            P("ep", None),
            P(),
            P("ep", None, "tp"),
            P("ep", None, "tp"),
            P("ep", "tp", None),
            P(),
        ),
        out_specs=(P(("ep", "tp"), None), P(("ep", "tp"), None)),
        check_vma=False,
    )
```
